32 devices in a mesh: pipe: 2 (over x), fsdp: 8 (over z, y), tp: 2 (over core).
Axes of the slice: x: 2, y: 2, z: 4, core: 2. Of those that a mesh axis runs over, the one named last changes fastest.
Arguments:
- inputs: bfloat16 [4, 512, 1152], P(None, ('fsdp', 'tp')), may hold values from -6 to 6
- cotangent: bfloat16 [4, 512, 1152], P(None, ('fsdp', 'tp')), may hold values from -6 to 6
- image_ids: int32 [4, 512], replicated, may hold values from 0 to 2, as said below
- proj_in: bfloat16 [2, 1152, 3, 1152], P('pipe', 'fsdp', None, 'tp'), may hold values from -0.1875 to 0.1875
- bias_in: bfloat16 [2, 2, 1152], P('pipe', None, 'tp'), may hold values from -3 to 3
- proj_out: bfloat16 [2, 1152, 1152], P('pipe', 'fsdp', 'tp'), may hold values from -3 to 3
- bias_out: bfloat16 [2, 1152], P('pipe'), may hold values from -3 to 3
- gain_attn: bfloat16 [2, 1152], P('pipe'), may hold values from 0.25 to 1.75
- shift_attn: bfloat16 [2, 1152], P('pipe'), may hold values from -2 to 2
- up_projection: bfloat16 [2, 1152, 4304], P('pipe', 'fsdp', 'tp'), may hold values from -0.1875 to 0.1875
- up_bias_vector: bfloat16 [2, 4304], P('pipe', 'tp'), may hold values from -3 to 3
- down_projection: bfloat16 [2, 1152, 4304], P('pipe', 'fsdp', 'tp'), may hold values from -0.09375 to 0.09375
- bias_down: bfloat16 [2, 1152], P('pipe'), may hold values from -3 to 3
- gain_feed: bfloat16 [2, 1152], P('pipe'), may hold values from 0.25 to 1.75
- shift_feed: bfloat16 [2, 1152], P('pipe'), may hold values from -2 to 2
Outputs:
- activations: bfloat16 [2, 4, 512, 1152], P('pipe', None, ('fsdp', 'tp'))
- grad_inputs: bfloat16 [2, 4, 512, 1152], P('pipe', None, ('fsdp', 'tp'))
- grad_proj_in: float32 [2, 1152, 3, 1152], P('pipe', 'fsdp', None, 'tp')
- grad_bias_in: float32 [2, 2, 1152], P('pipe', None, 'tp')
- grad_proj_out: float32 [2, 1152, 1152], P('pipe', 'fsdp', 'tp')
- grad_bias_out: float32 [2, 1152], P('pipe')
- grad_gain_attn: float32 [2, 1152], P('pipe')
- grad_shift_attn: float32 [2, 1152], P('pipe')
- grad_proj_up: float32 [2, 1152, 4304], P('pipe', 'fsdp', 'tp')
- grad_bias_up: float32 [2, 4304], P('pipe', 'tp')
- grad_proj_down: float32 [2, 1152, 4304], P('pipe', 'fsdp', 'tp')
- grad_bias_down: float32 [2, 1152], P('pipe')
- grad_gain_feed: float32 [2, 1152], P('pipe')
- grad_shift_feed: float32 [2, 1152], P('pipe')
The draws below stay inside these ranges and needn't reach their ends.
Inputs may be any that keep to these rules, and one draw needn't show every extreme that they name: `image_ids`: every image has 1 to 256 rows of its micro-batch, and one has exactly 256.
All inputs are finite; a program needn't handle non-finite values.
Results may differ from the reference program's by a relative error of at most 0.014.
Values may be sent and summed in bfloat16 or wider, within the bound.
No kernel may reach another device: no remote copies, remote signals or barrier semaphores. Data moves between devices by JAX's collectives and lax.ppermute only.
A program may use at most 256 MiB of HBM per device.

```python
import jax
import jax.numpy as jnp
from jax import lax

D = 1152
HEADS = 16
HD = 72
FF = 4304
SECTIONS = 2
MICRO = 4
TOK_DEV = 64
ROWS = 512
IMG_MOST = 256
IMAGES = 3


def draw_image_ids(key, part):
    rest_rows = ROWS - IMG_MOST
    others = IMAGES - 1
    share = rest_rows // others
    jitter = share // 8
    cuts_count = max(others - 1, 1)
    moves = jax.random.randint(key, (MICRO, cuts_count), -jitter, jitter + 1)
    cuts = (jnp.arange(1, cuts_count + 1, dtype=jnp.int32) * share)[None, :] + moves
    if others - 1 == 0:
        cuts = jnp.full((MICRO, 1), rest_rows + 1, jnp.int32)
    position = jnp.arange(ROWS, dtype=jnp.int32)
    offset = position - IMG_MOST
    later = 1 + jnp.sum((cuts[:, None, :] <= offset[None, :, None]).astype(jnp.int32), axis=-1)
    sorted_ids = jnp.where(position[None, :] < IMG_MOST, 0, later).astype(jnp.int32)
    blocks = ROWS // TOK_DEV
    source = position % TOK_DEV * blocks + position // TOK_DEV
    return jnp.take(sorted_ids, source, axis=1).astype(jnp.int32)


def shard_levels(rng, extent, shards, smallest, top_value):
    def one(dim, shards_of):
        heights = jax.random.uniform(jax.random.fold_in(jax.random.fold_in(rng, 6), dim), (shards_of,), jnp.float32, smallest / len(shards), top_value / len(shards))
        return jnp.repeat(jnp.exp(heights), extent[dim] // shards_of).reshape((-1,) + (1,) * (len(extent) - dim - 1))

    level = one(*shards[0])
    for cut in shards[1:]:
        level = level * one(*cut)
    return level


def scatter_about(own_key, extent, width, reach, shards=(), kind=jnp.bfloat16):
    array = jax.random.normal(own_key, extent, jnp.float32) * width
    if len(shards) > 0:
        array = shard_levels(own_key, extent, shards, -0.22, 0.18) * array
    return jnp.clip(array, min=-reach, max=reach).astype(kind)


def setup_inputs(seed: int = 0) -> dict:
    streams_of = jax.random.split(jax.random.key(seed), 16)
    return {
        "inputs": scatter_about(streams_of[0], (MICRO, ROWS, D), 1.0, 6.0, ((1, 16),)),
        "cotangent": scatter_about(streams_of[1], (MICRO, ROWS, D), 1.0, 6.0, ((1, 16),)),
        "image_ids": draw_image_ids(jax.random.fold_in(streams_of[15], 71), 0),
        "proj_in": scatter_about(streams_of[3], (SECTIONS, D, 3, D), D ** -0.5, 0.1875, ((0, 2), (1, 8), (3, 2))),
        "bias_in": scatter_about(streams_of[4], (SECTIONS, 2, D), 0.5, 3.0, ((0, 2), (2, 2))),
        "proj_out": scatter_about(streams_of[5], (SECTIONS, D, D), (max(D // 256, 1)) ** -0.5, 3.0, ((0, 2), (1, 8), (2, 2))),
        "bias_out": scatter_about(streams_of[6], (SECTIONS, D), 0.5, 3.0, ((0, 2),)),
        "gain_attn": jnp.clip(1.0 + 0.15 * jax.random.normal(streams_of[7], (SECTIONS, D), jnp.float32), 0.25, 1.75).astype(jnp.bfloat16),
        "shift_attn": scatter_about(streams_of[8], (SECTIONS, D), 0.3, 2.0, ((0, 2),)),
        "up_projection": scatter_about(streams_of[9], (SECTIONS, D, FF), D ** -0.5, 0.1875, ((0, 2), (1, 8), (2, 2))),
        "up_bias_vector": scatter_about(streams_of[10], (SECTIONS, FF), 0.5, 3.0, ((0, 2), (1, 2))),
        "down_projection": scatter_about(streams_of[11], (SECTIONS, D, FF), FF ** -0.5, 0.09375, ((0, 2), (1, 8), (2, 2))),
        "bias_down": scatter_about(streams_of[12], (SECTIONS, D), 0.5, 3.0, ((0, 2),)),
        "gain_feed": jnp.clip(1.0 + 0.15 * jax.random.normal(streams_of[13], (SECTIONS, D), jnp.float32), 0.25, 1.75).astype(jnp.bfloat16),
        "shift_feed": scatter_about(streams_of[14], (SECTIONS, D), 0.3, 2.0, ((0, 2),)),
    }


@jax.custom_vjp
def low(v):
    return lax.optimization_barrier(v.astype(jnp.bfloat16)).astype(jnp.float32)

@jax.custom_vjp
def low_back(v):
    return v

def low_keep(v):
    return (low(v), None)

def low_pass(kept, grad):
    return (grad,)

def back_keep(v):
    return (v, None)

def back_low(kept, grad):
    return (low(grad),)
low.defvjp(low_keep, low_pass)
low_back.defvjp(back_keep, back_low)
EPSILON = 1e-06
HIGH_ACCURACY = lax.Precision.HIGHEST
MASKED = -1e+30

def normalize(values, gain_vec, shift_vec):
    row_mean = lax.optimization_barrier(jnp.mean(values, axis=-1, keepdims=True))
    center = values - row_mean
    spread = lax.optimization_barrier(jnp.mean(center * center, axis=-1, keepdims=True))
    return center * lax.rsqrt(spread + EPSILON) * gain_vec + shift_vec

def head_attention(packed):
    query_h, keys_h, values_h, image_row = packed
    raw_scores = jnp.dot(query_h, keys_h.T, precision=HIGH_ACCURACY) * HD ** (-0.5)
    masked = jnp.where(image_row[:, None] == image_row[None, :], raw_scores, MASKED)
    masked = low_back(masked)
    row_max = lax.optimization_barrier(jnp.max(masked, axis=-1, keepdims=True))
    exp_scores = jnp.exp(masked - row_max)
    soft_probs = exp_scores / lax.optimization_barrier(jnp.sum(exp_scores, axis=-1, keepdims=True))
    return jnp.dot(low(soft_probs), values_h, precision=HIGH_ACCURACY)

def split_heads(values):
    return values.reshape(MICRO, ROWS, HEADS, HD).transpose(0, 2, 1, 3).reshape(MICRO * HEADS, ROWS, HD)

def join_heads(values):
    return values.reshape(MICRO, HEADS, ROWS, HD).transpose(0, 2, 1, 3).reshape(MICRO, ROWS, D)

def layer(hidden_in, image_ids, proj_in, bias_in, proj_out, bias_out, gain_attn, shift_attn, up_projection, up_bias_vector, down_projection, bias_down, gain_feed, shift_feed):
    normed = low(normalize(hidden_in, gain_attn, shift_attn))
    projected = jnp.einsum('mrd,dce->mrce', normed, proj_in, precision=HIGH_ACCURACY)
    query_all = low(low_back(projected[:, :, 0] + bias_in[0]))
    keys_all = low(low_back(projected[:, :, 1]))
    values_all = low(low_back(projected[:, :, 2] + bias_in[1]))
    id_rows = jnp.repeat(image_ids, HEADS, axis=0)
    context = lax.map(jax.checkpoint(head_attention), (split_heads(query_all), split_heads(keys_all), split_heads(values_all), id_rows))
    context = low(low_back(join_heads(context)))
    attended = low_back(jnp.einsum('mrj,dj->mrd', context, proj_out, precision=HIGH_ACCURACY))
    middle = hidden_in + attended + bias_out
    feed_input = low(normalize(middle, gain_feed, shift_feed))
    hidden_state = low_back(jnp.einsum('wlk,ka->wla', feed_input, up_projection, precision=HIGH_ACCURACY) + up_bias_vector)
    active_section = low(jax.nn.gelu(hidden_state, approximate=True))
    feed_output = low_back(jnp.einsum('oyc,wc->oyw', active_section, down_projection, precision=HIGH_ACCURACY))
    return middle + feed_output + bias_down

def reference(inputs, cotangent, image_ids, proj_in, bias_in, proj_out, bias_out, gain_attn, shift_attn, up_projection, up_bias_vector, down_projection, bias_down, gain_feed, shift_feed):
    weights = [w.astype(jnp.float32) for w in (proj_in, bias_in, proj_out, bias_out, gain_attn, shift_attn, up_projection, up_bias_vector, down_projection, bias_down, gain_feed, shift_feed)]
    first = [w[0] for w in weights]
    second = [w[1] for w in weights]

    def first_section(hidden_in, *params):
        return low(low_back(layer(hidden_in, image_ids, *params)))

    def second_section(hidden_in, *params):
        return layer(hidden_in, image_ids, *params)
    middle_act, first_back = jax.vjp(first_section, inputs.astype(jnp.float32), *first)
    final_act, second_back = jax.vjp(second_section, middle_act, *second)
    second_grads = second_back(cotangent.astype(jnp.float32))
    first_grads = first_back(second_grads[0])
    stacked = [jnp.stack((one_grad, two_grad)).astype(jnp.float32) for one_grad, two_grad in zip(first_grads[1:], second_grads[1:])]
    activations = jnp.stack((middle_act, final_act)).astype(jnp.bfloat16)
    grad_inputs = jnp.stack((first_grads[0], second_grads[0])).astype(jnp.bfloat16)
    return (activations, grad_inputs, stacked[0], stacked[1], stacked[2], stacked[3], stacked[4], stacked[5], stacked[6], stacked[7], stacked[8], stacked[9], stacked[10], stacked[11])
```

```python
import jax
import jax.numpy as jnp
from jax import lax
from jax.sharding import PartitionSpec as P

HD = 72
EPSILON = 1e-06
MASKED = -1e30


def from_behind(value, axis, steps):
    count = lax.axis_size(axis)
    initial, last = (max(0, -steps), min(count, count - steps))
    return lax.ppermute(value, axis, [(source, source + steps) for source in range(initial, last)])


def normalize(values, gain_vec, shift_vec):
    row_mean = jnp.mean(values, axis=-1, keepdims=True)
    center = values - row_mean
    spread = jnp.mean(center * center, axis=-1, keepdims=True)
    return center * lax.rsqrt(spread + EPSILON) * gain_vec + shift_vec


def gelu_tanh(values):
    return jax.nn.gelu(values, approximate=True)


def rows_gather(values):
    return lax.all_gather(values, "tp", axis=0, tiled=True)


def rows_reduce(values):
    return lax.psum_scatter(values, "tp", scatter_dimension=0, tiled=True)


def grad_gather(values):
    return lax.all_gather(values, "tp", axis=0, tiled=True)


def grad_reduce(values):
    return lax.psum_scatter(values, "tp", scatter_dimension=0, tiled=True)


def contract_last(left, right):
    return lax.dot_general(
        left, right, (((1,), (1,)), ((), ())), preferred_element_type=jnp.float32
    )


def head_scores(query_low, keys_all, same_image, heads_local):
    query_h = query_low.reshape(query_low.shape[0], heads_local, HD)
    keys_h = keys_all.reshape(keys_all.shape[0], heads_local, HD)
    raw_scores = jnp.einsum(
        "qhe,khe->hqk", query_h, keys_h, preferred_element_type=jnp.float32
    ) * HD ** (-0.5)
    return jnp.where(same_image[None], raw_scores, MASKED)


def put_slot(buffer, value, slot_num):
    return lax.dynamic_update_index_in_dim(buffer, value, slot_num, 0)


def get_slot(buffer, slot_num):
    return lax.dynamic_index_in_dim(buffer, slot_num, 0, keepdims=False)


def body(
    inputs,
    cotangent,
    image_ids,
    proj_in,
    bias_in,
    proj_out,
    bias_out,
    gain_attn,
    shift_attn,
    up_projection,
    up_bias_vector,
    down_projection,
    bias_down,
    gain_feed,
    shift_feed,
):
    micro_count = inputs.shape[0]
    half_rows = inputs.shape[1]
    model_width = inputs.shape[2]
    local_cols = proj_in.shape[3]
    heads_local = local_cols // HD
    hidden_cols = up_projection.shape[2]
    section_num = lax.axis_index("pipe")
    block_num = lax.axis_index("fsdp")
    tok_rows = half_rows * lax.axis_size("tp")
    all_rows = tok_rows * lax.axis_size("fsdp")
    slot_count = micro_count + 1
    score_scale = HD ** (-0.5)
    weight_in, weight_out, weight_up, weight_down = (
        lax.all_gather(proj_in[0], "fsdp", axis=0, tiled=True),
        lax.all_gather(proj_out[0], "fsdp", axis=0, tiled=True),
        lax.all_gather(up_projection[0], "fsdp", axis=0, tiled=True),
        lax.all_gather(down_projection[0], "fsdp", axis=0, tiled=True),
    )
    qv_bias = bias_in[0].astype(jnp.float32)
    out_shift = bias_out[0].astype(jnp.float32)
    attn_gain = gain_attn[0].astype(jnp.float32)
    attn_shift = shift_attn[0].astype(jnp.float32)
    up_shift = up_bias_vector[0].astype(jnp.float32)
    down_shift = bias_down[0].astype(jnp.float32)
    feed_gain = gain_feed[0].astype(jnp.float32)
    feed_shift = shift_feed[0].astype(jnp.float32)
    keep_input = jnp.zeros((slot_count, half_rows, model_width), jnp.float32)
    keep_middle = jnp.zeros((slot_count, half_rows, model_width), jnp.float32)
    keep_normed = jnp.zeros((slot_count, tok_rows, model_width), jnp.bfloat16)
    keep_query = jnp.zeros((slot_count, tok_rows, local_cols), jnp.bfloat16)
    keep_keys = jnp.zeros((slot_count, all_rows, local_cols), jnp.bfloat16)
    keep_values = jnp.zeros((slot_count, all_rows, local_cols), jnp.bfloat16)
    keep_lse = jnp.zeros((slot_count, heads_local, tok_rows), jnp.float32)
    keep_context = jnp.zeros((slot_count, tok_rows, local_cols), jnp.bfloat16)
    keep_feed = jnp.zeros((slot_count, tok_rows, model_width), jnp.bfloat16)
    keep_hidden = jnp.zeros((slot_count, tok_rows, hidden_cols), jnp.float32)
    act_store = jnp.zeros((slot_count, half_rows, model_width), jnp.bfloat16)
    received = jnp.zeros((half_rows, model_width), jnp.bfloat16)
    for step_num in range(micro_count + 1):
        index_mb = step_num - section_num
        slot_num = (index_mb + slot_count) % slot_count
        take_num = jnp.clip(index_mb, 0, micro_count - 1)
        fresh_rows = get_slot(inputs, take_num)
        rows_now = jnp.where(section_num == 0, fresh_rows, received).astype(jnp.float32)
        batch_ids = get_slot(image_ids, take_num)
        query_ids = lax.dynamic_slice_in_dim(batch_ids, block_num * tok_rows, tok_rows)
        same_image = query_ids[:, None] == batch_ids[None, :]
        normed = rows_gather(normalize(rows_now, attn_gain, attn_shift).astype(jnp.bfloat16))
        projected = jnp.einsum("rd,dce->rce", normed, weight_in, preferred_element_type=jnp.float32)
        query_low = (projected[:, 0] + qv_bias[0]).astype(jnp.bfloat16)
        keys_own = projected[:, 1].astype(jnp.bfloat16)
        values_own = (projected[:, 2] + qv_bias[1]).astype(jnp.bfloat16)
        keys_all, values_all = (
            lax.all_gather(keys_own, "fsdp", axis=0, tiled=True),
            lax.all_gather(values_own, "fsdp", axis=0, tiled=True),
        )
        scores = head_scores(query_low, keys_all, same_image, heads_local)
        row_max = jnp.max(scores, axis=-1, keepdims=True)
        exp_scores = jnp.exp(scores - row_max)
        row_total = jnp.sum(exp_scores, axis=-1, keepdims=True)
        soft_probs = (exp_scores / row_total).astype(jnp.bfloat16)
        log_total = (row_max + jnp.log(row_total))[:, :, 0]
        context = jnp.einsum(
            "hqk,khe->qhe",
            soft_probs,
            values_all.reshape(all_rows, heads_local, HD),
            preferred_element_type=jnp.float32,
        )
        context = context.reshape(tok_rows, local_cols).astype(jnp.bfloat16)
        middle = rows_now + rows_reduce(contract_last(context, weight_out)) + out_shift
        feed_input = rows_gather(normalize(middle, feed_gain, feed_shift).astype(jnp.bfloat16))
        hidden_state = jnp.dot(feed_input, weight_up, preferred_element_type=jnp.float32) + up_shift
        active_section = gelu_tanh(hidden_state).astype(jnp.bfloat16)
        result = middle + rows_reduce(contract_last(active_section, weight_down)) + down_shift
        result_low = result.astype(jnp.bfloat16)
        keep_input = put_slot(keep_input, rows_now, slot_num)
        keep_middle = put_slot(keep_middle, middle, slot_num)
        keep_normed = put_slot(keep_normed, normed, slot_num)
        keep_query = put_slot(keep_query, query_low, slot_num)
        keep_keys = put_slot(keep_keys, keys_all, slot_num)
        keep_values = put_slot(keep_values, values_all, slot_num)
        keep_lse = put_slot(keep_lse, log_total, slot_num)
        keep_context = put_slot(keep_context, context, slot_num)
        keep_feed = put_slot(keep_feed, feed_input, slot_num)
        keep_hidden = put_slot(keep_hidden, hidden_state, slot_num)
        act_store = put_slot(act_store, result_low, slot_num)
        if step_num < micro_count:
            received = from_behind(result_low, "pipe", 1)
    totals = (
        jnp.zeros(weight_in.shape, jnp.float32),
        jnp.zeros(weight_out.shape, jnp.float32),
        jnp.zeros(weight_up.shape, jnp.float32),
        jnp.zeros(weight_down.shape, jnp.float32),
    )
    qv_total = jnp.zeros((2, local_cols), jnp.float32)
    up_total = jnp.zeros((hidden_cols,), jnp.float32)
    vector_totals = tuple((jnp.zeros((model_width,), jnp.float32) for index_vec in range(6)))
    grad_store = jnp.zeros((slot_count, half_rows, model_width), jnp.bfloat16)
    incoming = jnp.zeros((half_rows, model_width), jnp.bfloat16)
    for step_num in range(micro_count + 1):
        index_mb = step_num - 1 + section_num
        valid_mask = jnp.logical_and(index_mb >= 0, index_mb < micro_count).astype(jnp.float32)
        slot_num = (index_mb + slot_count) % slot_count
        take_num = jnp.clip(index_mb, 0, micro_count - 1)
        given = get_slot(cotangent, take_num)
        grad_out = jnp.where(section_num == 1, given, incoming).astype(jnp.float32)
        batch_ids = get_slot(image_ids, take_num)
        query_ids = lax.dynamic_slice_in_dim(batch_ids, block_num * tok_rows, tok_rows)
        same_image = query_ids[:, None] == batch_ids[None, :]
        rows_now = get_slot(keep_input, slot_num)
        middle = get_slot(keep_middle, slot_num)
        normed = get_slot(keep_normed, slot_num)
        query_low = get_slot(keep_query, slot_num)
        log_total = get_slot(keep_lse, slot_num)
        context = get_slot(keep_context, slot_num)
        feed_input = get_slot(keep_feed, slot_num)
        hidden_state = get_slot(keep_hidden, slot_num)
        keys_all = get_slot(keep_keys, slot_num)
        values_all = get_slot(keep_values, slot_num)
        down_grad = grad_gather(grad_out.astype(jnp.bfloat16))
        active_section = gelu_tanh(hidden_state).astype(jnp.bfloat16)
        grad_down_w = jnp.einsum(
            "rd,rf->df", down_grad, active_section, preferred_element_type=jnp.float32
        )
        active_grad = jnp.dot(down_grad, weight_down, preferred_element_type=jnp.float32)
        gelu_value, gelu_back = jax.vjp(gelu_tanh, hidden_state)
        hidden_grad = gelu_back(active_grad)[0].astype(jnp.bfloat16)
        grad_up_w = jnp.einsum(
            "rd,rf->df", feed_input, hidden_grad, preferred_element_type=jnp.float32
        )
        feed_grad = grad_reduce(contract_last(hidden_grad, weight_up))
        feed_value, feed_back = jax.vjp(normalize, middle, feed_gain, feed_shift)
        middle_part, feed_gain_grad, feed_shift_grad = feed_back(feed_grad)
        middle_grad = grad_out + middle_part
        attn_grad = grad_gather(middle_grad.astype(jnp.bfloat16))
        grad_out_w = jnp.einsum("rd,rj->dj", attn_grad, context, preferred_element_type=jnp.float32)
        context_grad = jnp.dot(attn_grad, weight_out, preferred_element_type=jnp.float32).astype(
            jnp.bfloat16
        )
        scores = head_scores(query_low, keys_all, same_image, heads_local)
        soft_probs = jnp.exp(scores - log_total[:, :, None])
        context_h = context_grad.reshape(tok_rows, heads_local, HD)
        values_h = values_all.reshape(all_rows, heads_local, HD)
        keys_h = keys_all.reshape(all_rows, heads_local, HD)
        query_h = query_low.reshape(tok_rows, heads_local, HD)
        prob_grad = jnp.einsum(
            "qhe,khe->hqk", context_h, values_h, preferred_element_type=jnp.float32
        )
        inner = jnp.sum(soft_probs * prob_grad, axis=-1, keepdims=True)
        score_grad = (soft_probs * (prob_grad - inner)).astype(jnp.bfloat16)
        query_grad = (
            jnp.einsum("hqk,khe->qhe", score_grad, keys_h, preferred_element_type=jnp.float32)
            * score_scale
        )
        query_grad = query_grad.reshape(tok_rows, local_cols).astype(jnp.bfloat16)
        key_part = (
            jnp.einsum("hqk,qhe->khe", score_grad, query_h, preferred_element_type=jnp.float32)
            * score_scale
        ).reshape(all_rows, local_cols)
        value_part = jnp.einsum(
            "hqk,qhe->khe",
            soft_probs.astype(jnp.bfloat16),
            context_h,
            preferred_element_type=jnp.float32,
        ).reshape(all_rows, local_cols)
        key_sum, value_sum = (
            lax.psum_scatter(key_part, "fsdp", scatter_dimension=0, tiled=True),
            lax.psum_scatter(value_part, "fsdp", scatter_dimension=0, tiled=True),
        )
        key_grad = key_sum.astype(jnp.bfloat16)
        value_grad = value_sum.astype(jnp.bfloat16)
        joined = jnp.stack((query_grad, key_grad, value_grad), axis=1)
        grad_in_w = jnp.einsum("rd,rce->dce", normed, joined, preferred_element_type=jnp.float32)
        normed_grad = grad_reduce(
            jnp.einsum("rce,dce->rd", joined, weight_in, preferred_element_type=jnp.float32)
        )
        attn_value, attn_back = jax.vjp(normalize, rows_now, attn_gain, attn_shift)
        rows_part, attn_gain_grad, attn_shift_grad = attn_back(normed_grad)
        input_grad = (middle_grad + rows_part).astype(jnp.bfloat16)
        grad_store = put_slot(grad_store, input_grad, slot_num)
        qv_step = jnp.stack(
            (
                jnp.sum(query_grad.astype(jnp.float32), axis=0),
                jnp.sum(value_grad.astype(jnp.float32), axis=0),
            )
        )
        qv_total = qv_total + valid_mask * qv_step
        up_total = up_total + valid_mask * jnp.sum(hidden_grad.astype(jnp.float32), axis=0)
        vector_steps = (
            jnp.sum(middle_grad, axis=0),
            attn_gain_grad,
            attn_shift_grad,
            jnp.sum(grad_out, axis=0),
            feed_gain_grad,
            feed_shift_grad,
        )
        vector_totals = tuple(
            (
                old_vec + valid_mask * new_vec
                for old_vec, new_vec in zip(vector_totals, vector_steps)
            )
        )
        step_in = valid_mask * grad_in_w
        step_out = valid_mask * grad_out_w
        step_up = valid_mask * grad_up_w
        step_down = valid_mask * grad_down_w
        totals = (
            totals[0] + step_in,
            totals[1] + step_out,
            totals[2] + step_up,
            totals[3] + step_down,
        )
        if step_num < micro_count:
            incoming = from_behind(input_grad, "pipe", -1)
    totals = (
        lax.psum_scatter(totals[0], "fsdp", scatter_dimension=0, tiled=True),
        lax.psum_scatter(totals[1], "fsdp", scatter_dimension=0, tiled=True),
        lax.psum_scatter(totals[2], "fsdp", scatter_dimension=0, tiled=True),
        lax.psum_scatter(totals[3], "fsdp", scatter_dimension=0, tiled=True),
    )
    qv_sum, up_sum = lax.psum((qv_total, up_total), "fsdp")
    vector_sums = lax.psum(
        (
            vector_totals[0],
            vector_totals[1],
            vector_totals[2],
            vector_totals[3],
            vector_totals[4],
            vector_totals[5],
        ),
        ("fsdp", "tp"),
    )
    return (
        act_store[:micro_count][None],
        grad_store[:micro_count][None],
        totals[0][None],
        qv_sum[None],
        totals[1][None],
        vector_sums[0][None],
        vector_sums[1][None],
        vector_sums[2][None],
        totals[2][None],
        up_sum[None],
        totals[3][None],
        vector_sums[3][None],
        vector_sums[4][None],
        vector_sums[5][None],
    )


LANES = 128


def swap_pairs(count, step):
    return [(at, at ^ step) for at in range(count)]


def pick(take_first, first, second):
    return jnp.where(take_first, first, second)


class Plane:
    def __init__(self, planes):
        self.groups = lax.axis_size("fsdp")
        self.planes = planes
        self.across = lax.axis_index("pipe")
        place = lax.axis_index("fsdp")
        self.near = self.groups // planes
        self.plane = place // self.near
        self.side = place % self.near
        self.core = lax.axis_index("tp")

    def pipe(self, value):
        return lax.ppermute(value, "pipe", [(0, 1), (1, 0)])

    def beside(self, value):
        return lax.ppermute(value, "fsdp", swap_pairs(self.groups, 1))

    def corner(self, value):
        pairs = [
            (one * self.groups + at, (1 - one) * self.groups + (at ^ 1))
            for one in range(2)
            for at in range(self.groups)
        ]
        return lax.ppermute(value, ("pipe", "fsdp"), pairs)

    def core_swap(self, value):
        return lax.ppermute(value, "tp", [(0, 1), (1, 0)])

    def plane_shift(self, value, steps):
        pairs = [(at, (at + steps * self.near) % self.groups) for at in range(self.groups)]
        return lax.ppermute(value, "fsdp", pairs)

    def plane_lists(self):
        return [
            [plane * self.near + side for plane in range(self.planes)] for side in range(self.near)
        ]

    def gather_rows(self, own):
        mine = jnp.concatenate((own, self.pipe(own), self.beside(own), self.corner(own)), axis=0)
        return jnp.concatenate((mine, self.core_swap(mine)), axis=0)

    def reduce_rows(self, partial):
        half = partial.shape[0] // 2
        quarter = half // 4
        low = jnp.bfloat16
        chip = partial[:half] + self.core_swap(partial[half:].astype(low)).astype(jnp.float32)
        low_chip = chip.astype(low)
        return (
            chip[:quarter]
            + self.pipe(low_chip[quarter : 2 * quarter]).astype(jnp.float32)
            + self.beside(low_chip[2 * quarter : 3 * quarter]).astype(jnp.float32)
            + self.corner(low_chip[3 * quarter :]).astype(jnp.float32)
        )

    def relative(self, parts, axis_note=None):
        p00, p01, p10, p11 = parts
        up = self.across == 0
        self_0, self_1 = pick(up, p00, p10), pick(up, p01, p11)
        other_0, other_1 = pick(up, p10, p00), pick(up, p11, p01)
        first = self.side == 0
        return (
            pick(first, self_0, self_1),
            pick(first, other_0, other_1),
            pick(first, self_1, self_0),
            pick(first, other_1, other_0),
        )

    def absolute(self, parts):
        one, pipe, beside, corner = parts
        first = self.side == 0
        self_0, self_1 = pick(first, one, beside), pick(first, beside, one)
        other_0, other_1 = pick(first, pipe, corner), pick(first, corner, pipe)
        up = self.across == 0
        return (
            pick(up, self_0, other_0),
            pick(up, self_1, other_1),
            pick(up, other_0, self_0),
            pick(up, other_1, self_1),
        )

    def spread_weight(self, shard):
        one, pipe, beside, corner = self.relative([shard[:, at] for at in range(4)])
        pipe, beside, corner = self.pipe(pipe), self.beside(beside), self.corner(corner)
        first = self.side == 0
        same = jnp.concatenate((pick(first, one, beside), pick(first, beside, one)), axis=0)
        other = jnp.concatenate((pick(first, pipe, corner), pick(first, corner, pipe)), axis=0)
        up = self.across == 0
        return pick(up, same, other), pick(up, other, same)

    def gather_planes(self, value):
        return lax.all_gather(
            value, "fsdp", axis=0, tiled=True, axis_index_groups=self.plane_lists()
        )

    def reduce_planes(self, value):
        return lax.psum_scatter(
            value, "fsdp", scatter_dimension=0, tiled=True, axis_index_groups=self.plane_lists()
        )

    def collect_weight(self, first_section, second_section):
        rows = first_section.shape[0] // 2
        up = self.across == 0
        same, other = pick(up, first_section, second_section), pick(up, second_section, first_section)
        first = self.side == 0
        parts = (
            pick(first, same[:rows], same[rows:]),
            self.pipe(pick(first, other[:rows], other[rows:])),
            self.beside(pick(first, same[rows:], same[:rows])),
            self.corner(pick(first, other[rows:], other[:rows])),
        )
        return self.absolute(parts)

    def rows_in(self, value):
        got = [lax.dynamic_index_in_dim(value, self.plane, 0, keepdims=False)]
        for steps in range(1, self.planes):
            target = (self.plane + steps) % self.planes
            sent = lax.dynamic_index_in_dim(value, target, 0, keepdims=False)
            got.append(self.plane_shift(sent, steps))
        return self.turned(got)

    def turned(self, got):
        stacked = jnp.stack(got)
        order = [(self.plane + self.planes - at) % self.planes for at in range(self.planes)]
        return jnp.stack(
            [lax.dynamic_index_in_dim(stacked, at, 0, keepdims=False) for at in order]
        )

    def halves(self, value):
        half = self.planes // 2
        flat = value.reshape(2, half * value.shape[1], value.shape[2])
        up = self.across == 0
        return pick(up, flat[0], flat[1]), pick(up, flat[1], flat[0])

    def rows_out(self, first_section, second_section):
        up = self.across == 0
        kept = pick(up, first_section, second_section)
        came = self.pipe(pick(up, second_section, first_section))
        both = jnp.concatenate((pick(up, kept, came), pick(up, came, kept)), axis=0)
        blocks = both.reshape(self.planes, both.shape[0] // self.planes, both.shape[1])
        return self.rows_in(blocks)


def norm_parts(values):
    row_mean = jnp.mean(values, axis=-1, keepdims=True)
    center = values - row_mean
    spread = jnp.mean(center * center, axis=-1, keepdims=True)
    scale = lax.rsqrt(spread + EPSILON)
    return center * scale, scale


def norm_forward(values, gain_vec, shift_vec):
    return norm_parts(values)[0] * gain_vec + shift_vec


def norm_backward(values, gain_vec, grad):
    shape, scale = norm_parts(values)
    inner = grad * gain_vec
    mean_one = jnp.mean(inner, axis=-1, keepdims=True)
    mean_two = jnp.mean(inner * shape, axis=-1, keepdims=True)
    back = (inner - mean_one - shape * mean_two) * scale
    return back, jnp.sum(grad * shape, axis=0), jnp.sum(grad, axis=0)


def mul(left, right):
    return jnp.dot(left, right, preferred_element_type=jnp.float32)


def mul_first(left, right):
    return lax.dot_general(left, right, (((0,), (0,)), ((), ())), preferred_element_type=jnp.float32)


def pad_heads(value, parts, lanes):
    lead = value.shape[:-1]
    split = value.reshape(lead + (parts, HD))
    wide = jnp.pad(split, [(0, 0)] * len(lead) + [(0, 0), (0, lanes - HD)])
    return wide.reshape(lead + (parts * lanes,))


def unpad_heads(value, parts, lanes):
    return jnp.concatenate(
        [value[..., at * lanes : at * lanes + HD] for at in range(parts)], axis=-1
    )


def gelu_both(values):
    root = (2.0 / jnp.pi) ** 0.5
    square = values * values
    inside = jnp.tanh(root * values * (1.0 + 0.044715 * square))
    value = 0.5 * values * (1.0 + inside)
    slope = 0.5 * (1.0 + inside) + 0.5 * values * (1.0 - inside * inside) * root * (
        1.0 + 3.0 * 0.044715 * square
    )
    return value, slope


def attend(query, keys, values, same_image):
    scores = contract_last(query, keys) * HD ** (-0.5)
    scores = jnp.where(same_image, scores, MASKED)
    row_max = jnp.max(scores, axis=-1, keepdims=True)
    exp_scores = jnp.exp(scores - row_max)
    probs = exp_scores / jnp.sum(exp_scores, axis=-1, keepdims=True)
    return mul(probs.astype(jnp.bfloat16), values), probs


def attend_back(query, keys, values, probs, context_grad):
    prob_grad = contract_last(context_grad, values)
    inner = jnp.sum(probs * prob_grad, axis=-1, keepdims=True)
    score_grad = (probs * (prob_grad - inner)).astype(jnp.bfloat16)
    scale = HD ** (-0.5)
    return (
        mul(score_grad, keys) * scale,
        mul_first(score_grad, query) * scale,
        mul_first(probs.astype(jnp.bfloat16), context_grad),
    )


class Section:
    def __init__(self, plane, heads, weights, vectors):
        self.plane = plane
        self.heads = heads
        into, out, self.up, self.down = weights
        self.into = pad_heads(into, 3 * heads, LANES)
        self.out = pad_heads(out, heads, LANES)
        (
            self.query_bias,
            self.value_bias,
            self.up_bias,
            self.out_bias,
            self.gain_attn,
            self.shift_attn,
            self.down_bias,
            self.gain_feed,
            self.shift_feed,
        ) = vectors

    def norm_attn(self, rows):
        return norm_forward(rows, self.gain_attn, self.shift_attn).astype(jnp.bfloat16)

    def head(self, value, at):
        return value[:, at * LANES : (at + 1) * LANES]

    def forward(self, rows, normed, same_image, last):
        plane, heads = self.plane, self.heads
        width = heads * LANES
        self.rows, self.normed, self.same_image = rows, normed, same_image
        projected = mul(normed, self.into)
        self.query = (projected[:, :width] + self.query_bias).astype(jnp.bfloat16)
        self.keys = projected[:, width : 2 * width].astype(jnp.bfloat16)
        self.values = (projected[:, 2 * width :] + self.value_bias).astype(jnp.bfloat16)
        context, self.probs = [], []
        for at in range(heads):
            one, probs = attend(
                self.head(self.query, at), self.head(self.keys, at), self.head(self.values, at), same_image
            )
            context.append(one.astype(jnp.bfloat16))
            self.probs.append(probs)
        self.context = jnp.concatenate(context, axis=1)
        self.middle = rows + plane.reduce_rows(contract_last(self.context, self.out)) + self.out_bias
        feed = norm_forward(self.middle, self.gain_feed, self.shift_feed).astype(jnp.bfloat16)
        self.feed = plane.gather_rows(feed)
        self.hidden = mul(self.feed, self.up) + self.up_bias
        self.active = gelu_both(self.hidden)[0].astype(jnp.bfloat16)
        fed = plane.reduce_rows(contract_last(self.active, self.down))
        return (self.middle + fed + self.down_bias).astype(jnp.bfloat16)

    def backward(self, grad, gathered):
        plane, heads = self.plane, self.heads
        low = jnp.bfloat16
        grad_down = mul_first(gathered, self.active).astype(low)
        active_grad = mul(gathered, self.down)
        hidden_grad = (active_grad * gelu_both(self.hidden)[1]).astype(low)
        feed_grad = plane.reduce_rows(contract_last(hidden_grad, self.up))
        grad_up = mul_first(self.feed, hidden_grad).astype(low)
        grad_up_bias = jnp.sum(hidden_grad.astype(jnp.float32), axis=0)
        back, grad_gain_feed, grad_shift_feed = norm_backward(self.middle, self.gain_feed, feed_grad)
        middle_grad = grad + back
        attn_grad = plane.gather_rows(middle_grad.astype(low))
        context_grad = mul(attn_grad, self.out).astype(low)
        grad_out = mul_first(attn_grad, self.context)
        grads = [[], [], []]
        for at in range(heads):
            parts = attend_back(
                self.head(self.query, at),
                self.head(self.keys, at),
                self.head(self.values, at),
                self.probs[at],
                self.head(context_grad, at),
            )
            for kept, part in zip(grads, parts):
                kept.append(part.astype(low))
        joined = jnp.concatenate(grads[0] + grads[1] + grads[2], axis=1)
        normed_grad = plane.reduce_rows(contract_last(joined, self.into))
        grad_in = mul_first(self.normed, joined)
        wide_sums = jnp.sum(joined.astype(jnp.float32), axis=0)
        rows_back, grad_gain_attn, grad_shift_attn = norm_backward(self.rows, self.gain_attn, normed_grad)
        result = (middle_grad + rows_back).astype(low)
        weights = (
            unpad_heads(grad_in.astype(low), 3 * heads, LANES),
            unpad_heads(grad_out.astype(low), heads, LANES),
            grad_up,
            grad_down,
        )
        sums = (
            jnp.sum(middle_grad, axis=0),
            grad_gain_attn,
            grad_shift_attn,
            jnp.sum(grad, axis=0),
            grad_gain_feed,
            grad_shift_feed,
        )
        bias_sums = unpad_heads(wide_sums, 3 * heads, LANES)
        own = heads * HD
        columns = jnp.concatenate((bias_sums[:own], bias_sums[2 * own :], grad_up_bias))
        return result, weights, sums, columns


def plane_body(
    inputs,
    cotangent,
    image_ids,
    proj_in,
    bias_in,
    proj_out,
    bias_out,
    gain_attn,
    shift_attn,
    up_projection,
    up_bias_vector,
    down_projection,
    bias_down,
    gain_feed,
    shift_feed,
):
    micro_count, part_rows, model_width = inputs.shape
    local_cols = proj_in.shape[3]
    hidden_cols = up_projection.shape[2]
    shard_rows = proj_in.shape[1]
    plane = Plane(micro_count)
    shares = 4
    own_cols = local_cols // shares
    own_hidden = hidden_cols // shares
    heads = own_cols // HD
    up = plane.across == 0
    share_num = plane.across * 2 + plane.side

    rows_all = plane.rows_in(inputs)

    tail = -hidden_cols % model_width
    vec = jnp.concatenate(
        [bias_in[0].reshape(-1), bias_out[0], gain_attn[0], shift_attn[0], bias_down[0], gain_feed[0], shift_feed[0]]
        + [up_bias_vector[0], jnp.zeros((tail,), jnp.bfloat16)]
    ).reshape(-1, model_width)
    vec_other = plane.pipe(vec)

    def vectors(section):
        chosen = pick(up == (section == 0), vec, vec_other).astype(jnp.float32)
        query_all = chosen[0, :local_cols].reshape(shares, own_cols)
        value_all = chosen[0, local_cols:].reshape(shares, own_cols)
        hidden_all = chosen[7:].reshape(-1)[:hidden_cols].reshape(shares, own_hidden)
        mine = [
            lax.dynamic_index_in_dim(one, share_num, 0, keepdims=False)
            for one in (query_all, value_all, hidden_all)
        ]
        wide = [pad_heads(one, heads, LANES) for one in mine[:2]]
        return (wide[0], wide[1], mine[2]) + tuple(chosen[at] for at in range(1, 7))

    split_in = jnp.swapaxes(proj_in[0].reshape(shard_rows, 3, shares, own_cols), 1, 2).reshape(
        shard_rows, shares, 3 * own_cols
    )
    shards = (
        split_in,
        proj_out[0].reshape(shard_rows, shares, own_cols),
        up_projection[0].reshape(shard_rows, shares, own_hidden),
        down_projection[0].reshape(shard_rows, shares, own_hidden),
    )
    spread = [plane.spread_weight(shard) for shard in shards]
    whole = [[plane.gather_planes(pair[section]) for pair in spread] for section in range(2)]
    sections = [Section(plane, heads, whole[section], vectors(section)) for section in range(2)]

    ids = lax.dynamic_index_in_dim(image_ids, plane.plane, 0, keepdims=False)
    ids = ids.reshape(2, micro_count // 2, 2, 2, part_rows)
    ids = pick(up, ids, jnp.flip(ids, 0))
    ids = pick(plane.side == 0, ids, jnp.flip(ids, 2))
    ids = pick(plane.core == 0, ids, jnp.flip(ids, 3))
    ids = ids.transpose(3, 2, 0, 1, 4).reshape(-1)
    same_image = ids[:, None] == ids[None, :]

    own_rows, pair_rows = plane.halves(rows_all)
    first = sections[0]
    pair_normed = first.norm_attn(jnp.concatenate((own_rows, pair_rows), axis=0).astype(jnp.float32))
    mine = jnp.concatenate((pair_normed, plane.beside(pair_normed)), axis=0)
    normed = jnp.concatenate((mine, plane.core_swap(mine)), axis=0)
    result = []
    rows = own_rows
    for section in range(2):
        one = sections[section]
        rows = rows.astype(jnp.float32)
        if section > 0:
            normed = plane.gather_rows(one.norm_attn(rows))
        rows = one.forward(rows, normed, same_image, section == 1)
        result.append(rows)

    given = plane.rows_in(cotangent)
    own_given, pair_given = plane.halves(given)
    pair = jnp.concatenate((own_given, pair_given), axis=0)
    mine = jnp.concatenate((pair, plane.beside(pair)), axis=0)
    gathered = jnp.concatenate((mine, plane.core_swap(mine)), axis=0)
    grad = own_given
    back = [None, None]
    weight_grads, sums, columns = [None, None], [None, None], [None, None]
    for section in (1, 0):
        if section == 0:
            gathered = plane.gather_rows(grad)
        grad, weights, sums[section], columns[section] = sections[section].backward(
            grad.astype(jnp.float32), gathered
        )
        back[section] = grad
        weight_grads[section] = [plane.reduce_planes(one) for one in weights]

    activations = plane.rows_out(result[0], result[1])
    grad_inputs = plane.rows_out(back[0], back[1])
    blocks = [
        plane.collect_weight(one, two) for one, two in zip(weight_grads[0], weight_grads[1])
    ]
    blocks = [[part.astype(jnp.float32) for part in four] for four in blocks]
    grad_in = jnp.concatenate(
        [part.reshape(shard_rows, 3, own_cols) for part in blocks[0]], axis=2
    )
    grad_out, grad_up, grad_down = [jnp.concatenate(four, axis=1) for four in blocks[1:]]

    column_count = columns[0].shape[0]
    pad = -column_count % model_width
    packs = [
        jnp.concatenate(sums[section] + (columns[section], jnp.zeros((pad,), jnp.float32))).reshape(-1, model_width)
        for section in range(2)
    ]
    pack = jnp.concatenate(packs, axis=0)
    both = pack + plane.core_swap(pack)
    per = packs[0].shape[0]
    rolled = jnp.stack([both[:6], both[per : per + 6]])
    held = jnp.stack([pack[6:per], pack[per + 6 :]])
    message = jnp.concatenate((rolled, held), axis=1)
    send_same = pick(up, message[0], message[1])
    send_other = pick(up, message[1], message[0])
    parts = (send_same, plane.pipe(send_other), plane.beside(send_same), plane.corner(send_other))
    ordered = plane.absolute(parts)
    total = parts[0][:6] + parts[1][:6] + parts[2][:6] + parts[3][:6]
    kept = jnp.concatenate([total] + [part[6:] for part in ordered], axis=0)
    full = kept
    for steps in range(1, plane.planes):
        full = full + plane.plane_shift(kept, steps)
    parts = full[6:].reshape(shares, -1)[:, :column_count]
    grad_bias_in = jnp.stack(
        (parts[:, :own_cols].reshape(-1), parts[:, own_cols : 2 * own_cols].reshape(-1))
    )
    grad_up_bias = parts[:, 2 * own_cols :].reshape(-1)
    return (
        activations[None],
        grad_inputs[None],
        grad_in[None],
        grad_bias_in[None],
        grad_out[None],
        full[0][None],
        full[1][None],
        full[2][None],
        grad_up[None],
        grad_up_bias[None],
        grad_down[None],
        full[3][None],
        full[4][None],
        full[5][None],
    )


def fits_planes(inputs, proj_in, up_projection):
    micro_count = inputs.shape[0]
    return (
        lax.axis_size("pipe") == 2
        and lax.axis_size("tp") == 2
        and micro_count % 2 == 0
        and lax.axis_size("fsdp") == 2 * micro_count
        and proj_in.shape[3] % (4 * HD) == 0
        and up_projection.shape[2] % 4 == 0
    )


def choose(inputs, cotangent, image_ids, proj_in, *rest):
    form = plane_body if fits_planes(inputs, proj_in, rest[5]) else body
    return form(inputs, cotangent, image_ids, proj_in, *rest)


def solution(mesh):
    placed = (
        P(None, ("fsdp", "tp"), None),
        P(None, ("fsdp", "tp"), None),
        P(),
        P("pipe", "fsdp", None, "tp"),
        P("pipe", None, "tp"),
        P("pipe", "fsdp", "tp"),
        P("pipe", None),
        P("pipe", None),
        P("pipe", None),
        P("pipe", "fsdp", "tp"),
        P("pipe", "tp"),
        P("pipe", "fsdp", "tp"),
        P("pipe", None),
        P("pipe", None),
        P("pipe", None),
    )
    return jax.shard_map(
        choose,
        mesh=mesh,
        in_specs=placed,
        out_specs=(
            P("pipe", None, ("fsdp", "tp"), None),
            P("pipe", None, ("fsdp", "tp"), None),
            P("pipe", "fsdp", None, "tp"),
            P("pipe", None, "tp"),
            P("pipe", "fsdp", "tp"),
            P("pipe", None),
            P("pipe", None),
            P("pipe", None),
            P("pipe", "fsdp", "tp"),
            P("pipe", "tp"),
            P("pipe", "fsdp", "tp"),
            P("pipe", None),
            P("pipe", None),
            P("pipe", None),
        ),
        check_vma=False,
    )
```

```python
import jax
import jax.numpy as jnp
from jax import lax
from jax.sharding import PartitionSpec as P

HD = 72
EPSILON = 1e-06
MASKED = -1e30


def from_behind(value, axis, steps):
    count = lax.axis_size(axis)
    initial, last = (max(0, -steps), min(count, count - steps))
    return lax.ppermute(value, axis, [(source, source + steps) for source in range(initial, last)])


def normalize(values, gain_vec, shift_vec):
    row_mean = jnp.mean(values, axis=-1, keepdims=True)
    center = values - row_mean
    spread = jnp.mean(center * center, axis=-1, keepdims=True)
    return center * lax.rsqrt(spread + EPSILON) * gain_vec + shift_vec


def gelu_tanh(values):
    return jax.nn.gelu(values, approximate=True)


def rows_gather(values):
    return lax.all_gather(values, "tp", axis=0, tiled=True)


def rows_reduce(values):
    return lax.psum_scatter(values, "tp", scatter_dimension=0, tiled=True)


def grad_gather(values):
    return lax.all_gather(values, "tp", axis=0, tiled=True)


def grad_reduce(values):
    return lax.psum_scatter(values, "tp", scatter_dimension=0, tiled=True)


def contract_last(left, right):
    return lax.dot_general(
        left, right, (((1,), (1,)), ((), ())), preferred_element_type=jnp.float32
    )


def head_scores(query_low, keys_all, same_image, heads_local):
    query_h = query_low.reshape(query_low.shape[0], heads_local, HD)
    keys_h = keys_all.reshape(keys_all.shape[0], heads_local, HD)
    raw_scores = jnp.einsum(
        "qhe,khe->hqk", query_h, keys_h, preferred_element_type=jnp.float32
    ) * HD ** (-0.5)
    return jnp.where(same_image[None], raw_scores, MASKED)


def put_slot(buffer, value, slot_num):
    return lax.dynamic_update_index_in_dim(buffer, value, slot_num, 0)


def get_slot(buffer, slot_num):
    return lax.dynamic_index_in_dim(buffer, slot_num, 0, keepdims=False)


def body(
    inputs,
    cotangent,
    image_ids,
    proj_in,
    bias_in,
    proj_out,
    bias_out,
    gain_attn,
    shift_attn,
    up_projection,
    up_bias_vector,
    down_projection,
    bias_down,
    gain_feed,
    shift_feed,
):
    micro_count = inputs.shape[0]
    half_rows = inputs.shape[1]
    model_width = inputs.shape[2]
    local_cols = proj_in.shape[3]
    heads_local = local_cols // HD
    hidden_cols = up_projection.shape[2]
    section_num = lax.axis_index("pipe")
    block_num = lax.axis_index("fsdp")
    tok_rows = half_rows * lax.axis_size("tp")
    all_rows = tok_rows * lax.axis_size("fsdp")
    slot_count = micro_count + 1
    score_scale = HD ** (-0.5)
    weight_in, weight_out, weight_up, weight_down = (
        lax.all_gather(proj_in[0], "fsdp", axis=0, tiled=True),
        lax.all_gather(proj_out[0], "fsdp", axis=0, tiled=True),
        lax.all_gather(up_projection[0], "fsdp", axis=0, tiled=True),
        lax.all_gather(down_projection[0], "fsdp", axis=0, tiled=True),
    )
    qv_bias = bias_in[0].astype(jnp.float32)
    out_shift = bias_out[0].astype(jnp.float32)
    attn_gain = gain_attn[0].astype(jnp.float32)
    attn_shift = shift_attn[0].astype(jnp.float32)
    up_shift = up_bias_vector[0].astype(jnp.float32)
    down_shift = bias_down[0].astype(jnp.float32)
    feed_gain = gain_feed[0].astype(jnp.float32)
    feed_shift = shift_feed[0].astype(jnp.float32)
    keep_input = jnp.zeros((slot_count, half_rows, model_width), jnp.float32)
    keep_middle = jnp.zeros((slot_count, half_rows, model_width), jnp.float32)
    keep_normed = jnp.zeros((slot_count, tok_rows, model_width), jnp.bfloat16)
    keep_query = jnp.zeros((slot_count, tok_rows, local_cols), jnp.bfloat16)
    keep_keys = jnp.zeros((slot_count, all_rows, local_cols), jnp.bfloat16)
    keep_values = jnp.zeros((slot_count, all_rows, local_cols), jnp.bfloat16)
    keep_lse = jnp.zeros((slot_count, heads_local, tok_rows), jnp.float32)
    keep_context = jnp.zeros((slot_count, tok_rows, local_cols), jnp.bfloat16)
    keep_feed = jnp.zeros((slot_count, tok_rows, model_width), jnp.bfloat16)
    keep_hidden = jnp.zeros((slot_count, tok_rows, hidden_cols), jnp.float32)
    act_store = jnp.zeros((slot_count, half_rows, model_width), jnp.bfloat16)
    received = jnp.zeros((half_rows, model_width), jnp.bfloat16)
    for step_num in range(micro_count + 1):
        index_mb = step_num - section_num
        slot_num = (index_mb + slot_count) % slot_count
        take_num = jnp.clip(index_mb, 0, micro_count - 1)
        fresh_rows = get_slot(inputs, take_num)
        rows_now = jnp.where(section_num == 0, fresh_rows, received).astype(jnp.float32)
        batch_ids = get_slot(image_ids, take_num)
        query_ids = lax.dynamic_slice_in_dim(batch_ids, block_num * tok_rows, tok_rows)
        same_image = query_ids[:, None] == batch_ids[None, :]
        normed = rows_gather(normalize(rows_now, attn_gain, attn_shift).astype(jnp.bfloat16))
        projected = jnp.einsum("rd,dce->rce", normed, weight_in, preferred_element_type=jnp.float32)
        query_low = (projected[:, 0] + qv_bias[0]).astype(jnp.bfloat16)
        keys_own = projected[:, 1].astype(jnp.bfloat16)
        values_own = (projected[:, 2] + qv_bias[1]).astype(jnp.bfloat16)
        keys_all, values_all = (
            lax.all_gather(keys_own, "fsdp", axis=0, tiled=True),
            lax.all_gather(values_own, "fsdp", axis=0, tiled=True),
        )
        scores = head_scores(query_low, keys_all, same_image, heads_local)
        row_max = jnp.max(scores, axis=-1, keepdims=True)
        exp_scores = jnp.exp(scores - row_max)
        row_total = jnp.sum(exp_scores, axis=-1, keepdims=True)
        soft_probs = (exp_scores / row_total).astype(jnp.bfloat16)
        log_total = (row_max + jnp.log(row_total))[:, :, 0]
        context = jnp.einsum(
            "hqk,khe->qhe",
            soft_probs,
            values_all.reshape(all_rows, heads_local, HD),
            preferred_element_type=jnp.float32,
        )
        context = context.reshape(tok_rows, local_cols).astype(jnp.bfloat16)
        middle = rows_now + rows_reduce(contract_last(context, weight_out)) + out_shift
        feed_input = rows_gather(normalize(middle, feed_gain, feed_shift).astype(jnp.bfloat16))
        hidden_state = jnp.dot(feed_input, weight_up, preferred_element_type=jnp.float32) + up_shift
        active_section = gelu_tanh(hidden_state).astype(jnp.bfloat16)
        result = middle + rows_reduce(contract_last(active_section, weight_down)) + down_shift
        result_low = result.astype(jnp.bfloat16)
        keep_input = put_slot(keep_input, rows_now, slot_num)
        keep_middle = put_slot(keep_middle, middle, slot_num)
        keep_normed = put_slot(keep_normed, normed, slot_num)
        keep_query = put_slot(keep_query, query_low, slot_num)
        keep_keys = put_slot(keep_keys, keys_all, slot_num)
        keep_values = put_slot(keep_values, values_all, slot_num)
        keep_lse = put_slot(keep_lse, log_total, slot_num)
        keep_context = put_slot(keep_context, context, slot_num)
        keep_feed = put_slot(keep_feed, feed_input, slot_num)
        keep_hidden = put_slot(keep_hidden, hidden_state, slot_num)
        act_store = put_slot(act_store, result_low, slot_num)
        if step_num < micro_count:
            received = from_behind(result_low, "pipe", 1)
    totals = (
        jnp.zeros(weight_in.shape, jnp.float32),
        jnp.zeros(weight_out.shape, jnp.float32),
        jnp.zeros(weight_up.shape, jnp.float32),
        jnp.zeros(weight_down.shape, jnp.float32),
    )
    qv_total = jnp.zeros((2, local_cols), jnp.float32)
    up_total = jnp.zeros((hidden_cols,), jnp.float32)
    vector_totals = tuple((jnp.zeros((model_width,), jnp.float32) for index_vec in range(6)))
    grad_store = jnp.zeros((slot_count, half_rows, model_width), jnp.bfloat16)
    incoming = jnp.zeros((half_rows, model_width), jnp.bfloat16)
    for step_num in range(micro_count + 1):
        index_mb = step_num - 1 + section_num
        valid_mask = jnp.logical_and(index_mb >= 0, index_mb < micro_count).astype(jnp.float32)
        slot_num = (index_mb + slot_count) % slot_count
        take_num = jnp.clip(index_mb, 0, micro_count - 1)
        given = get_slot(cotangent, take_num)
        grad_out = jnp.where(section_num == 1, given, incoming).astype(jnp.float32)
        batch_ids = get_slot(image_ids, take_num)
        query_ids = lax.dynamic_slice_in_dim(batch_ids, block_num * tok_rows, tok_rows)
        same_image = query_ids[:, None] == batch_ids[None, :]
        rows_now = get_slot(keep_input, slot_num)
        middle = get_slot(keep_middle, slot_num)
        normed = get_slot(keep_normed, slot_num)
        query_low = get_slot(keep_query, slot_num)
        log_total = get_slot(keep_lse, slot_num)
        context = get_slot(keep_context, slot_num)
        feed_input = get_slot(keep_feed, slot_num)
        hidden_state = get_slot(keep_hidden, slot_num)
        keys_all = get_slot(keep_keys, slot_num)
        values_all = get_slot(keep_values, slot_num)
        down_grad = grad_gather(grad_out.astype(jnp.bfloat16))
        active_section = gelu_tanh(hidden_state).astype(jnp.bfloat16)
        grad_down_w = jnp.einsum(
            "rd,rf->df", down_grad, active_section, preferred_element_type=jnp.float32
        )
        active_grad = jnp.dot(down_grad, weight_down, preferred_element_type=jnp.float32)
        gelu_value, gelu_back = jax.vjp(gelu_tanh, hidden_state)
        hidden_grad = gelu_back(active_grad)[0].astype(jnp.bfloat16)
        grad_up_w = jnp.einsum(
            "rd,rf->df", feed_input, hidden_grad, preferred_element_type=jnp.float32
        )
        feed_grad = grad_reduce(contract_last(hidden_grad, weight_up))
        feed_value, feed_back = jax.vjp(normalize, middle, feed_gain, feed_shift)
        middle_part, feed_gain_grad, feed_shift_grad = feed_back(feed_grad)
        middle_grad = grad_out + middle_part
        attn_grad = grad_gather(middle_grad.astype(jnp.bfloat16))
        grad_out_w = jnp.einsum("rd,rj->dj", attn_grad, context, preferred_element_type=jnp.float32)
        context_grad = jnp.dot(attn_grad, weight_out, preferred_element_type=jnp.float32).astype(
            jnp.bfloat16
        )
        scores = head_scores(query_low, keys_all, same_image, heads_local)
        soft_probs = jnp.exp(scores - log_total[:, :, None])
        context_h = context_grad.reshape(tok_rows, heads_local, HD)
        values_h = values_all.reshape(all_rows, heads_local, HD)
        keys_h = keys_all.reshape(all_rows, heads_local, HD)
        query_h = query_low.reshape(tok_rows, heads_local, HD)
        prob_grad = jnp.einsum(
            "qhe,khe->hqk", context_h, values_h, preferred_element_type=jnp.float32
        )
        inner = jnp.sum(soft_probs * prob_grad, axis=-1, keepdims=True)
        score_grad = (soft_probs * (prob_grad - inner)).astype(jnp.bfloat16)
        query_grad = (
            jnp.einsum("hqk,khe->qhe", score_grad, keys_h, preferred_element_type=jnp.float32)
            * score_scale
        )
        query_grad = query_grad.reshape(tok_rows, local_cols).astype(jnp.bfloat16)
        key_part = (
            jnp.einsum("hqk,qhe->khe", score_grad, query_h, preferred_element_type=jnp.float32)
            * score_scale
        ).reshape(all_rows, local_cols)
        value_part = jnp.einsum(
            "hqk,qhe->khe",
            soft_probs.astype(jnp.bfloat16),
            context_h,
            preferred_element_type=jnp.float32,
        ).reshape(all_rows, local_cols)
        key_sum, value_sum = (
            lax.psum_scatter(key_part, "fsdp", scatter_dimension=0, tiled=True),
            lax.psum_scatter(value_part, "fsdp", scatter_dimension=0, tiled=True),
        )
        key_grad = key_sum.astype(jnp.bfloat16)
        value_grad = value_sum.astype(jnp.bfloat16)
        joined = jnp.stack((query_grad, key_grad, value_grad), axis=1)
        grad_in_w = jnp.einsum("rd,rce->dce", normed, joined, preferred_element_type=jnp.float32)
        normed_grad = grad_reduce(
            jnp.einsum("rce,dce->rd", joined, weight_in, preferred_element_type=jnp.float32)
        )
        attn_value, attn_back = jax.vjp(normalize, rows_now, attn_gain, attn_shift)
        rows_part, attn_gain_grad, attn_shift_grad = attn_back(normed_grad)
        input_grad = (middle_grad + rows_part).astype(jnp.bfloat16)
        grad_store = put_slot(grad_store, input_grad, slot_num)
        qv_step = jnp.stack(
            (
                jnp.sum(query_grad.astype(jnp.float32), axis=0),
                jnp.sum(value_grad.astype(jnp.float32), axis=0),
            )
        )
        qv_total = qv_total + valid_mask * qv_step
        up_total = up_total + valid_mask * jnp.sum(hidden_grad.astype(jnp.float32), axis=0)
        vector_steps = (
            jnp.sum(middle_grad, axis=0),
            attn_gain_grad,
            attn_shift_grad,
            jnp.sum(grad_out, axis=0),
            feed_gain_grad,
            feed_shift_grad,
        )
        vector_totals = tuple(
            (
                old_vec + valid_mask * new_vec
                for old_vec, new_vec in zip(vector_totals, vector_steps)
            )
        )
        step_in = valid_mask * grad_in_w
        step_out = valid_mask * grad_out_w
        step_up = valid_mask * grad_up_w
        step_down = valid_mask * grad_down_w
        totals = (
            totals[0] + step_in,
            totals[1] + step_out,
            totals[2] + step_up,
            totals[3] + step_down,
        )
        if step_num < micro_count:
            incoming = from_behind(input_grad, "pipe", -1)
    totals = (
        lax.psum_scatter(totals[0], "fsdp", scatter_dimension=0, tiled=True),
        lax.psum_scatter(totals[1], "fsdp", scatter_dimension=0, tiled=True),
        lax.psum_scatter(totals[2], "fsdp", scatter_dimension=0, tiled=True),
        lax.psum_scatter(totals[3], "fsdp", scatter_dimension=0, tiled=True),
    )
    qv_sum, up_sum = lax.psum((qv_total, up_total), "fsdp")
    vector_sums = lax.psum(
        (
            vector_totals[0],
            vector_totals[1],
            vector_totals[2],
            vector_totals[3],
            vector_totals[4],
            vector_totals[5],
        ),
        ("fsdp", "tp"),
    )
    return (
        act_store[:micro_count][None],
        grad_store[:micro_count][None],
        totals[0][None],
        qv_sum[None],
        totals[1][None],
        vector_sums[0][None],
        vector_sums[1][None],
        vector_sums[2][None],
        totals[2][None],
        up_sum[None],
        totals[3][None],
        vector_sums[3][None],
        vector_sums[4][None],
        vector_sums[5][None],
    )


LANES = 128


def swap_pairs(count, step):
    return [(at, at ^ step) for at in range(count)]


def pick(take_first, first, second):
    return jnp.where(take_first, first, second)


class Plane:
    def __init__(self, planes):
        self.groups = lax.axis_size("fsdp")
        self.planes = planes
        self.across = lax.axis_index("pipe")
        place = lax.axis_index("fsdp")
        self.near = self.groups // planes
        self.plane = place // self.near
        self.side = place % self.near
        self.core = lax.axis_index("tp")

    def pipe(self, value):
        return lax.ppermute(value, "pipe", [(0, 1), (1, 0)])

    def beside(self, value):
        return lax.ppermute(value, "fsdp", swap_pairs(self.groups, 1))

    def corner(self, value):
        pairs = [
            (one * self.groups + at, (1 - one) * self.groups + (at ^ 1))
            for one in range(2)
            for at in range(self.groups)
        ]
        return lax.ppermute(value, ("pipe", "fsdp"), pairs)

    def core_swap(self, value):
        return lax.ppermute(value, "tp", [(0, 1), (1, 0)])

    def plane_shift(self, value, steps):
        pairs = [(at, (at + steps * self.near) % self.groups) for at in range(self.groups)]
        return lax.ppermute(value, "fsdp", pairs)

    def plane_lists(self):
        return [
            [plane * self.near + side for plane in range(self.planes)] for side in range(self.near)
        ]

    def gather_rows(self, own):
        mine = jnp.concatenate((own, self.pipe(own), self.beside(own), self.corner(own)), axis=0)
        return jnp.concatenate((mine, self.core_swap(mine)), axis=0)

    def reduce_rows(self, partial, beside=()):
        half = partial.shape[0] // 2
        quarter = half // 4
        low = jnp.bfloat16
        chip = partial[:half] + self.core_swap(partial[half:].astype(low)).astype(jnp.float32)
        low_chip = chip.astype(low)
        came = (
            self.pipe(low_chip[quarter : 2 * quarter]),
            self.beside(low_chip[2 * quarter : 3 * quarter]),
            self.corner(low_chip[3 * quarter :]),
        )
        came, beside = lax.optimization_barrier((came, beside))
        total = chip[:quarter]
        for part in came:
            total = total + part.astype(jnp.float32)
        return total, beside

    def absolute(self, parts):
        one, pipe, beside, corner = parts
        first = self.side == 0
        self_0, self_1 = pick(first, one, beside), pick(first, beside, one)
        other_0, other_1 = pick(first, pipe, corner), pick(first, corner, pipe)
        up = self.across == 0
        return (
            pick(up, self_0, other_0),
            pick(up, self_1, other_1),
            pick(up, other_0, self_0),
            pick(up, other_1, self_1),
        )

    def share(self, chunks, pipe_step, side_step):
        across = self.across if pipe_step == 0 else 1 - self.across
        side = self.side if side_step == 0 else 1 - self.side
        return lax.dynamic_index_in_dim(chunks, across * 2 + side, 0, keepdims=False)

    def spread_parts(self, chunks):
        return [self.share(chunks, pipe_step, side_step) for side_step in range(2) for pipe_step in range(2)]

    def spread_weight(self, parts):
        one, pipe, beside, corner = parts
        pipe, beside, corner = self.pipe(pipe), self.beside(beside), self.corner(corner)
        first = self.side == 0
        same = jnp.concatenate((pick(first, one, beside), pick(first, beside, one)), axis=0)
        other = jnp.concatenate((pick(first, pipe, corner), pick(first, corner, pipe)), axis=0)
        up = self.across == 0
        return pick(up, same, other), pick(up, other, same)

    def gather_planes(self, value):
        return lax.all_gather(
            value, "fsdp", axis=0, tiled=True, axis_index_groups=self.plane_lists()
        )

    def reduce_planes(self, value):
        return lax.psum_scatter(
            value, "fsdp", scatter_dimension=0, tiled=True, axis_index_groups=self.plane_lists()
        )

    def collect_weight(self, first_section, second_section):
        rows = first_section.shape[0] // 2
        up = self.across == 0
        same, other = pick(up, first_section, second_section), pick(up, second_section, first_section)
        first = self.side == 0
        parts = (
            pick(first, same[:rows], same[rows:]),
            self.pipe(pick(first, other[:rows], other[rows:])),
            self.beside(pick(first, same[rows:], same[:rows])),
            self.corner(pick(first, other[rows:], other[:rows])),
        )
        return self.absolute(parts)

    def rows_in(self, value):
        got = [lax.dynamic_index_in_dim(value, self.plane, 0, keepdims=False)]
        for steps in range(1, self.planes):
            target = (self.plane + steps) % self.planes
            sent = lax.dynamic_index_in_dim(value, target, 0, keepdims=False)
            got.append(self.plane_shift(sent, steps))
        return self.turned(got)

    def turned(self, got):
        stacked = jnp.stack(got)
        order = [(self.plane + self.planes - at) % self.planes for at in range(self.planes)]
        return jnp.stack(
            [lax.dynamic_index_in_dim(stacked, at, 0, keepdims=False) for at in order]
        )

    def halves(self, value):
        half = self.planes // 2
        flat = value.reshape(2, half * value.shape[1], value.shape[2])
        up = self.across == 0
        return pick(up, flat[0], flat[1]), pick(up, flat[1], flat[0])

    def rows_out(self, first_section, second_section):
        up = self.across == 0
        kept = pick(up, first_section, second_section)
        came = self.pipe(pick(up, second_section, first_section))
        both = jnp.concatenate((pick(up, kept, came), pick(up, came, kept)), axis=0)
        blocks = both.reshape(self.planes, both.shape[0] // self.planes, both.shape[1])
        return self.rows_in(blocks)


def norm_parts(values):
    row_mean = jnp.mean(values, axis=-1, keepdims=True)
    center = values - row_mean
    spread = jnp.mean(center * center, axis=-1, keepdims=True)
    scale = lax.rsqrt(spread + EPSILON)
    return center * scale, scale


def norm_forward(values, gain_vec, shift_vec):
    return norm_parts(values)[0] * gain_vec + shift_vec


def norm_backward(values, gain_vec, grad):
    shape, scale = norm_parts(values)
    inner = grad * gain_vec
    mean_one = jnp.mean(inner, axis=-1, keepdims=True)
    mean_two = jnp.mean(inner * shape, axis=-1, keepdims=True)
    back = (inner - mean_one - shape * mean_two) * scale
    return back, jnp.sum(grad * shape, axis=0), jnp.sum(grad, axis=0)


def mul(left, right):
    return jnp.dot(left, right, preferred_element_type=jnp.float32)


def mul_first(left, right):
    return lax.dot_general(left, right, (((0,), (0,)), ((), ())), preferred_element_type=jnp.float32)


def pad_heads(value, parts, lanes):
    lead = value.shape[:-1]
    split = value.reshape(lead + (parts, HD))
    wide = jnp.pad(split, [(0, 0)] * len(lead) + [(0, 0), (0, lanes - HD)])
    return wide.reshape(lead + (parts * lanes,))


def unpad_heads(value, parts, lanes):
    return jnp.concatenate(
        [value[..., at * lanes : at * lanes + HD] for at in range(parts)], axis=-1
    )


def gelu_both(values):
    root = (2.0 / jnp.pi) ** 0.5
    square = values * values
    inside = jnp.tanh(root * values * (1.0 + 0.044715 * square))
    value = 0.5 * values * (1.0 + inside)
    slope = 0.5 * (1.0 + inside) + 0.5 * values * (1.0 - inside * inside) * root * (
        1.0 + 3.0 * 0.044715 * square
    )
    return value, slope


def attend(query, keys, values, same_image):
    scores = contract_last(query, keys) * HD ** (-0.5)
    scores = jnp.where(same_image, scores, MASKED)
    row_max = jnp.max(scores, axis=-1, keepdims=True)
    exp_scores = jnp.exp(scores - row_max)
    probs = exp_scores / jnp.sum(exp_scores, axis=-1, keepdims=True)
    return mul(probs.astype(jnp.bfloat16), values), probs


def attend_back(query, keys, values, probs, context_grad):
    prob_grad = contract_last(context_grad, values)
    inner = jnp.sum(probs * prob_grad, axis=-1, keepdims=True)
    score_grad = (probs * (prob_grad - inner)).astype(jnp.bfloat16)
    scale = HD ** (-0.5)
    return (
        mul(score_grad, keys) * scale,
        mul_first(score_grad, query) * scale,
        mul_first(probs.astype(jnp.bfloat16), context_grad),
    )


class Section:
    def __init__(self, plane, heads, weights, vectors):
        self.plane = plane
        self.heads = heads
        attn, self.up, self.down = weights
        wide = pad_heads(attn, 4 * heads, LANES)
        self.into = wide[:, : 3 * heads * LANES]
        self.out = wide[:, 3 * heads * LANES :]
        (
            self.query_bias,
            self.value_bias,
            self.up_bias,
            self.out_bias,
            self.gain_attn,
            self.shift_attn,
            self.down_bias,
            self.gain_feed,
            self.shift_feed,
        ) = vectors

    def norm_attn(self, rows):
        return norm_forward(rows, self.gain_attn, self.shift_attn).astype(jnp.bfloat16)

    def head(self, value, at):
        return value[:, at * LANES : (at + 1) * LANES]

    def forward(self, rows, normed, same_image, last):
        plane, heads = self.plane, self.heads
        width = heads * LANES
        self.rows, self.normed, self.same_image = rows, normed, same_image
        projected = mul(normed, self.into)
        self.query = (projected[:, :width] + self.query_bias).astype(jnp.bfloat16)
        self.keys = projected[:, width : 2 * width].astype(jnp.bfloat16)
        self.values = (projected[:, 2 * width :] + self.value_bias).astype(jnp.bfloat16)
        context, self.probs = [], []
        for at in range(heads):
            one, probs = attend(
                self.head(self.query, at), self.head(self.keys, at), self.head(self.values, at), same_image
            )
            context.append(one.astype(jnp.bfloat16))
            self.probs.append(probs)
        self.context = jnp.concatenate(context, axis=1)
        attended, _ = plane.reduce_rows(contract_last(self.context, self.out))
        self.middle = rows + attended + self.out_bias
        feed = norm_forward(self.middle, self.gain_feed, self.shift_feed).astype(jnp.bfloat16)
        self.feed = plane.gather_rows(feed)
        self.hidden = mul(self.feed, self.up) + self.up_bias
        self.active = gelu_both(self.hidden)[0].astype(jnp.bfloat16)
        fed, _ = plane.reduce_rows(contract_last(self.active, self.down))
        return (self.middle + fed + self.down_bias).astype(jnp.bfloat16)

    def backward(self, grad, gathered, before=((), ())):
        plane, heads = self.plane, self.heads
        low = jnp.bfloat16
        rows_of = self.normed.shape[1] // (2 * plane.planes)
        active_grad = mul(gathered, self.down)
        hidden_grad = (active_grad * gelu_both(self.hidden)[1]).astype(low)
        grad_down = mul_first(gathered, self.active).astype(low)
        grad_up = mul_first(self.feed, hidden_grad).astype(low)
        split = (-1, 1, rows_of, grad_up.shape[1])
        grad_feed = jnp.concatenate((grad_up.reshape(split), grad_down.reshape(split)), axis=1)
        feed_grad, (grad_feed,) = plane.reduce_rows(contract_last(hidden_grad, self.up), (grad_feed,))
        feed_shard = plane.reduce_planes(grad_feed.reshape(-1, grad_up.shape[1]))
        grad_up_bias = jnp.sum(hidden_grad.astype(jnp.float32), axis=0)
        back, grad_gain_feed, grad_shift_feed = norm_backward(self.middle, self.gain_feed, feed_grad)
        middle_grad = grad + back
        low_middle, early = lax.optimization_barrier((middle_grad.astype(low), before[0]))
        attn_grad = plane.gather_rows(low_middle)
        context_grad = mul(attn_grad, self.out).astype(low)
        grads = [[], [], []]
        for at in range(heads):
            parts = attend_back(
                self.head(self.query, at),
                self.head(self.keys, at),
                self.head(self.values, at),
                self.probs[at],
                self.head(context_grad, at),
            )
            for kept, part in zip(grads, parts):
                kept.append(part.astype(low))
        joined = jnp.concatenate(grads[0] + grads[1] + grads[2], axis=1)
        grad_out = mul_first(attn_grad, self.context).astype(low)
        grad_in = mul_first(self.normed, joined).astype(low)
        grad_attn = unpad_heads(jnp.concatenate((grad_in, grad_out), axis=1), 4 * heads, LANES)
        normed_grad, (grad_attn,) = plane.reduce_rows(contract_last(joined, self.into), (grad_attn,))
        attn_shard = plane.reduce_planes(grad_attn)
        wide_sums = jnp.sum(joined.astype(jnp.float32), axis=0)
        normed_grad, late = lax.optimization_barrier((normed_grad, before[1]))
        rows_back, grad_gain_attn, grad_shift_attn = norm_backward(self.rows, self.gain_attn, normed_grad)
        result = (middle_grad + rows_back).astype(low)
        weights = (attn_shard, feed_shard)
        sums = (
            jnp.sum(middle_grad, axis=0),
            grad_gain_attn,
            grad_shift_attn,
            jnp.sum(grad, axis=0),
            grad_gain_feed,
            grad_shift_feed,
        )
        bias_sums = unpad_heads(wide_sums, 3 * heads, LANES)
        own = heads * HD
        columns = jnp.concatenate((bias_sums[:own], bias_sums[2 * own :], grad_up_bias))
        return result, weights, sums, columns, (early, late)


def plane_body(
    inputs,
    cotangent,
    image_ids,
    proj_in,
    bias_in,
    proj_out,
    bias_out,
    gain_attn,
    shift_attn,
    up_projection,
    up_bias_vector,
    down_projection,
    bias_down,
    gain_feed,
    shift_feed,
):
    micro_count, part_rows, model_width = inputs.shape
    local_cols = proj_in.shape[3]
    hidden_cols = up_projection.shape[2]
    shard_rows = proj_in.shape[1]
    plane = Plane(micro_count)
    shares = 4
    own_cols = local_cols // shares
    own_hidden = hidden_cols // shares
    heads = own_cols // HD
    up = plane.across == 0
    share_num = plane.across * 2 + plane.side

    attn = jnp.concatenate((proj_in[0], proj_out[0][:, None]), axis=1)
    attn = attn.reshape(shard_rows, 4, shares, own_cols).transpose(2, 0, 1, 3)
    attn_parts = plane.spread_parts(attn.reshape(shares, shard_rows, 4 * own_cols))

    lanes = hidden_cols
    vec = jnp.concatenate(
        [jnp.pad(one, ((0, 0), (0, lanes - one.shape[1]))) for one in (bias_in[0], bias_out, gain_attn)]
        + [jnp.pad(one, ((0, 0), (0, lanes - one.shape[1]))) for one in (shift_attn, bias_down, gain_feed)]
        + [jnp.pad(shift_feed, ((0, 0), (0, lanes - model_width))), up_bias_vector],
        axis=0,
    )
    attn_parts, vec, inputs = lax.optimization_barrier((attn_parts, vec, inputs))
    attn_pair = plane.spread_weight(attn_parts)
    vec_other = plane.pipe(vec)
    rows_all = plane.rows_in(inputs)

    attn_pair_now, up_projection, down_projection = lax.optimization_barrier(
        (attn_pair, up_projection, down_projection)
    )
    feed = jnp.concatenate((up_projection[0], down_projection[0]), axis=0)
    feed = feed.reshape(2 * shard_rows, shares, own_hidden).transpose(1, 0, 2)
    feed_pair = plane.spread_weight(plane.spread_parts(feed))

    vec_both = pick(up, jnp.stack((vec, vec_other)), jnp.stack((vec_other, vec))).astype(jnp.float32)
    bias_both = lax.dynamic_slice(vec_both, (0, 0, share_num * own_cols), (2, 2, own_cols))
    bias_both = pad_heads(bias_both, heads, LANES)
    hidden_both = lax.dynamic_slice(vec_both, (0, 8, share_num * own_hidden), (2, 1, own_hidden))

    def vectors(section):
        wide = vec_both[section, 2:8, :model_width]
        return (bias_both[section, :1], bias_both[section, 1:], hidden_both[section]) + tuple(
            wide[at : at + 1] for at in range(6)
        )

    def whole(section, attn_pair, feed_pair):
        attn_all = plane.gather_planes(attn_pair[section])
        feed_all = plane.gather_planes(feed_pair[section]).reshape(-1, 2, shard_rows, own_hidden)
        return (
            attn_all,
            feed_all[:, 0].reshape(-1, own_hidden),
            feed_all[:, 1].reshape(-1, own_hidden),
        )


    ids = lax.dynamic_index_in_dim(image_ids, plane.plane, 0, keepdims=False)
    ids = ids.reshape(2, micro_count // 2, 2, 2, part_rows)
    ids = pick(up, ids, jnp.flip(ids, 0))
    ids = pick(plane.side == 0, ids, jnp.flip(ids, 2))
    ids = pick(plane.core == 0, ids, jnp.flip(ids, 3))
    ids = ids.transpose(3, 2, 0, 1, 4).reshape(-1)
    same_image = ids[:, None] == ids[None, :]

    own_rows, pair_rows = plane.halves(rows_all)
    pair_float = jnp.concatenate((own_rows, pair_rows), axis=0).astype(jnp.float32)
    vector_sets = [vectors(section) for section in range(2)]
    pair_normed = norm_forward(pair_float, vector_sets[0][4], vector_sets[0][5]).astype(jnp.bfloat16)
    mine = jnp.concatenate((pair_normed, plane.beside(pair_normed)), axis=0)
    normed = jnp.concatenate((mine, plane.core_swap(mine)), axis=0)
    first_whole = whole(0, attn_pair, feed_pair)
    normed, attn_pair, feed_pair = lax.optimization_barrier((normed, attn_pair, feed_pair))
    sections = [
        Section(plane, heads, first_whole, vector_sets[0]),
        Section(plane, heads, whole(1, attn_pair, feed_pair), vector_sets[1]),
    ]
    result = []
    rows = own_rows
    for section in range(2):
        one = sections[section]
        rows = rows.astype(jnp.float32)
        if section > 0:
            normed = plane.gather_rows(one.norm_attn(rows))
        rows = one.forward(rows, normed, same_image, section == 1)
        result.append(rows)

    given = plane.rows_in(cotangent)
    own_given, pair_given = plane.halves(given)
    pair = jnp.concatenate((own_given, pair_given), axis=0)
    mine = jnp.concatenate((pair, plane.beside(pair)), axis=0)
    gathered = jnp.concatenate((mine, plane.core_swap(mine)), axis=0)
    grad = own_given
    back = [None, None]
    weight_grads, sums, columns = [None, None], [None, None], [None, None]
    for section in (1, 0):
        if section == 0:
            gathered = plane.gather_rows(grad)
        before = ((weight_grads[1][1],), (weight_grads[1][0],)) if section == 0 else ((), ())
        grad, weight_grads[section], sums[section], columns[section], held = sections[section].backward(
            grad.astype(jnp.float32), gathered, before
        )
        if section == 0:
            weight_grads[1] = (held[1][0], held[0][0])
        back[section] = grad

    activations = plane.rows_out(result[0], result[1])
    grad_inputs = plane.rows_out(back[0], back[1])
    blocks = [
        plane.collect_weight(one, two) for one, two in zip(weight_grads[0], weight_grads[1])
    ]
    blocks = [[part.astype(jnp.float32) for part in four] for four in blocks]
    split = (shard_rows, 4, own_cols)
    grad_attn = jnp.concatenate([part.reshape(split) for part in blocks[0]], axis=2)
    grad_in, grad_out = grad_attn[:, :3], grad_attn[:, 3]
    grad_feed = jnp.concatenate(blocks[1], axis=1)
    grad_up, grad_down = grad_feed[:shard_rows], grad_feed[shard_rows:]

    column_count = columns[0].shape[0]
    pad = -column_count % model_width
    packs = [
        jnp.concatenate(sums[section] + (columns[section], jnp.zeros((pad,), jnp.float32))).reshape(-1, model_width)
        for section in range(2)
    ]
    pack = jnp.concatenate(packs, axis=0)
    both = pack + plane.core_swap(pack)
    per = packs[0].shape[0]
    rolled = jnp.stack([both[:6], both[per : per + 6]])
    held = jnp.stack([pack[6:per], pack[per + 6 :]])
    message = jnp.concatenate((rolled, held), axis=1)
    send_same = pick(up, message[0], message[1])
    send_other = pick(up, message[1], message[0])
    parts = (send_same, plane.pipe(send_other), plane.beside(send_same), plane.corner(send_other))
    ordered = plane.absolute(parts)
    total = parts[0][:6] + parts[1][:6] + parts[2][:6] + parts[3][:6]
    kept = jnp.concatenate([total] + [part[6:] for part in ordered], axis=0)
    full = kept
    for steps in range(1, plane.planes):
        full = full + plane.plane_shift(kept, steps)
    parts = full[6:].reshape(shares, -1)[:, :column_count]
    grad_bias_in = jnp.stack(
        (parts[:, :own_cols].reshape(-1), parts[:, own_cols : 2 * own_cols].reshape(-1))
    )
    grad_up_bias = parts[:, 2 * own_cols :].reshape(-1)
    return (
        activations[None],
        grad_inputs[None],
        grad_in[None],
        grad_bias_in[None],
        grad_out[None],
        full[0][None],
        full[1][None],
        full[2][None],
        grad_up[None],
        grad_up_bias[None],
        grad_down[None],
        full[3][None],
        full[4][None],
        full[5][None],
    )


def fits_planes(inputs, proj_in, up_projection):
    micro_count = inputs.shape[0]
    return (
        lax.axis_size("pipe") == 2
        and lax.axis_size("tp") == 2
        and micro_count % 2 == 0
        and lax.axis_size("fsdp") == 2 * micro_count
        and proj_in.shape[3] % (4 * HD) == 0
        and up_projection.shape[2] % 4 == 0
    )


def choose(inputs, cotangent, image_ids, proj_in, *rest):
    form = plane_body if fits_planes(inputs, proj_in, rest[5]) else body
    return form(inputs, cotangent, image_ids, proj_in, *rest)


def solution(mesh):
    placed = (
        P(None, ("fsdp", "tp"), None),
        P(None, ("fsdp", "tp"), None),
        P(),
        P("pipe", "fsdp", None, "tp"),
        P("pipe", None, "tp"),
        P("pipe", "fsdp", "tp"),
        P("pipe", None),
        P("pipe", None),
        P("pipe", None),
        P("pipe", "fsdp", "tp"),
        P("pipe", "tp"),
        P("pipe", "fsdp", "tp"),
        P("pipe", None),
        P("pipe", None),
        P("pipe", None),
    )
    return jax.shard_map(
        choose,
        mesh=mesh,
        in_specs=placed,
        out_specs=(
            P("pipe", None, ("fsdp", "tp"), None),
            P("pipe", None, ("fsdp", "tp"), None),
            P("pipe", "fsdp", None, "tp"),
            P("pipe", None, "tp"),
            P("pipe", "fsdp", "tp"),
            P("pipe", None),
            P("pipe", None),
            P("pipe", None),
            P("pipe", "fsdp", "tp"),
            P("pipe", "tp"),
            P("pipe", "fsdp", "tp"),
            P("pipe", None),
            P("pipe", None),
            P("pipe", None),
        ),
        check_vma=False,
    )
```

```python
import functools

import jax
import jax.numpy as jnp
from jax import lax
from jax.experimental import pallas as pl
from jax.experimental.pallas import tpu as pltpu
from jax.sharding import PartitionSpec as P

HD = 72
EPSILON = 1e-06
MASKED = -1e30


def from_behind(value, axis, steps):
    count = lax.axis_size(axis)
    initial, last = (max(0, -steps), min(count, count - steps))
    return lax.ppermute(value, axis, [(source, source + steps) for source in range(initial, last)])


def normalize(values, gain_vec, shift_vec):
    row_mean = jnp.mean(values, axis=-1, keepdims=True)
    center = values - row_mean
    spread = jnp.mean(center * center, axis=-1, keepdims=True)
    return center * lax.rsqrt(spread + EPSILON) * gain_vec + shift_vec


def gelu_tanh(values):
    return jax.nn.gelu(values, approximate=True)


def rows_gather(values):
    return lax.all_gather(values, "tp", axis=0, tiled=True)


def rows_reduce(values):
    return lax.psum_scatter(values, "tp", scatter_dimension=0, tiled=True)


def grad_gather(values):
    return lax.all_gather(values, "tp", axis=0, tiled=True)


def grad_reduce(values):
    return lax.psum_scatter(values, "tp", scatter_dimension=0, tiled=True)


def contract_last(left, right):
    return lax.dot_general(
        left, right, (((1,), (1,)), ((), ())), preferred_element_type=jnp.float32
    )


def head_scores(query_low, keys_all, same_image, heads_local):
    query_h = query_low.reshape(query_low.shape[0], heads_local, HD)
    keys_h = keys_all.reshape(keys_all.shape[0], heads_local, HD)
    raw_scores = jnp.einsum(
        "qhe,khe->hqk", query_h, keys_h, preferred_element_type=jnp.float32
    ) * HD ** (-0.5)
    return jnp.where(same_image[None], raw_scores, MASKED)


def put_slot(buffer, value, slot_num):
    return lax.dynamic_update_index_in_dim(buffer, value, slot_num, 0)


def get_slot(buffer, slot_num):
    return lax.dynamic_index_in_dim(buffer, slot_num, 0, keepdims=False)


def body(
    inputs,
    cotangent,
    image_ids,
    proj_in,
    bias_in,
    proj_out,
    bias_out,
    gain_attn,
    shift_attn,
    up_projection,
    up_bias_vector,
    down_projection,
    bias_down,
    gain_feed,
    shift_feed,
):
    micro_count = inputs.shape[0]
    half_rows = inputs.shape[1]
    model_width = inputs.shape[2]
    local_cols = proj_in.shape[3]
    heads_local = local_cols // HD
    hidden_cols = up_projection.shape[2]
    section_num = lax.axis_index("pipe")
    block_num = lax.axis_index("fsdp")
    tok_rows = half_rows * lax.axis_size("tp")
    all_rows = tok_rows * lax.axis_size("fsdp")
    slot_count = micro_count + 1
    score_scale = HD ** (-0.5)
    weight_in, weight_out, weight_up, weight_down = (
        lax.all_gather(proj_in[0], "fsdp", axis=0, tiled=True),
        lax.all_gather(proj_out[0], "fsdp", axis=0, tiled=True),
        lax.all_gather(up_projection[0], "fsdp", axis=0, tiled=True),
        lax.all_gather(down_projection[0], "fsdp", axis=0, tiled=True),
    )
    qv_bias = bias_in[0].astype(jnp.float32)
    out_shift = bias_out[0].astype(jnp.float32)
    attn_gain = gain_attn[0].astype(jnp.float32)
    attn_shift = shift_attn[0].astype(jnp.float32)
    up_shift = up_bias_vector[0].astype(jnp.float32)
    down_shift = bias_down[0].astype(jnp.float32)
    feed_gain = gain_feed[0].astype(jnp.float32)
    feed_shift = shift_feed[0].astype(jnp.float32)
    keep_input = jnp.zeros((slot_count, half_rows, model_width), jnp.float32)
    keep_middle = jnp.zeros((slot_count, half_rows, model_width), jnp.float32)
    keep_normed = jnp.zeros((slot_count, tok_rows, model_width), jnp.bfloat16)
    keep_query = jnp.zeros((slot_count, tok_rows, local_cols), jnp.bfloat16)
    keep_keys = jnp.zeros((slot_count, all_rows, local_cols), jnp.bfloat16)
    keep_values = jnp.zeros((slot_count, all_rows, local_cols), jnp.bfloat16)
    keep_lse = jnp.zeros((slot_count, heads_local, tok_rows), jnp.float32)
    keep_context = jnp.zeros((slot_count, tok_rows, local_cols), jnp.bfloat16)
    keep_feed = jnp.zeros((slot_count, tok_rows, model_width), jnp.bfloat16)
    keep_hidden = jnp.zeros((slot_count, tok_rows, hidden_cols), jnp.float32)
    act_store = jnp.zeros((slot_count, half_rows, model_width), jnp.bfloat16)
    received = jnp.zeros((half_rows, model_width), jnp.bfloat16)
    for step_num in range(micro_count + 1):
        index_mb = step_num - section_num
        slot_num = (index_mb + slot_count) % slot_count
        take_num = jnp.clip(index_mb, 0, micro_count - 1)
        fresh_rows = get_slot(inputs, take_num)
        rows_now = jnp.where(section_num == 0, fresh_rows, received).astype(jnp.float32)
        batch_ids = get_slot(image_ids, take_num)
        query_ids = lax.dynamic_slice_in_dim(batch_ids, block_num * tok_rows, tok_rows)
        same_image = query_ids[:, None] == batch_ids[None, :]
        normed = rows_gather(normalize(rows_now, attn_gain, attn_shift).astype(jnp.bfloat16))
        projected = jnp.einsum("rd,dce->rce", normed, weight_in, preferred_element_type=jnp.float32)
        query_low = (projected[:, 0] + qv_bias[0]).astype(jnp.bfloat16)
        keys_own = projected[:, 1].astype(jnp.bfloat16)
        values_own = (projected[:, 2] + qv_bias[1]).astype(jnp.bfloat16)
        keys_all, values_all = (
            lax.all_gather(keys_own, "fsdp", axis=0, tiled=True),
            lax.all_gather(values_own, "fsdp", axis=0, tiled=True),
        )
        scores = head_scores(query_low, keys_all, same_image, heads_local)
        row_max = jnp.max(scores, axis=-1, keepdims=True)
        exp_scores = jnp.exp(scores - row_max)
        row_total = jnp.sum(exp_scores, axis=-1, keepdims=True)
        soft_probs = (exp_scores / row_total).astype(jnp.bfloat16)
        log_total = (row_max + jnp.log(row_total))[:, :, 0]
        context = jnp.einsum(
            "hqk,khe->qhe",
            soft_probs,
            values_all.reshape(all_rows, heads_local, HD),
            preferred_element_type=jnp.float32,
        )
        context = context.reshape(tok_rows, local_cols).astype(jnp.bfloat16)
        middle = rows_now + rows_reduce(contract_last(context, weight_out)) + out_shift
        feed_input = rows_gather(normalize(middle, feed_gain, feed_shift).astype(jnp.bfloat16))
        hidden_state = jnp.dot(feed_input, weight_up, preferred_element_type=jnp.float32) + up_shift
        active_section = gelu_tanh(hidden_state).astype(jnp.bfloat16)
        result = middle + rows_reduce(contract_last(active_section, weight_down)) + down_shift
        result_low = result.astype(jnp.bfloat16)
        keep_input = put_slot(keep_input, rows_now, slot_num)
        keep_middle = put_slot(keep_middle, middle, slot_num)
        keep_normed = put_slot(keep_normed, normed, slot_num)
        keep_query = put_slot(keep_query, query_low, slot_num)
        keep_keys = put_slot(keep_keys, keys_all, slot_num)
        keep_values = put_slot(keep_values, values_all, slot_num)
        keep_lse = put_slot(keep_lse, log_total, slot_num)
        keep_context = put_slot(keep_context, context, slot_num)
        keep_feed = put_slot(keep_feed, feed_input, slot_num)
        keep_hidden = put_slot(keep_hidden, hidden_state, slot_num)
        act_store = put_slot(act_store, result_low, slot_num)
        if step_num < micro_count:
            received = from_behind(result_low, "pipe", 1)
    totals = (
        jnp.zeros(weight_in.shape, jnp.float32),
        jnp.zeros(weight_out.shape, jnp.float32),
        jnp.zeros(weight_up.shape, jnp.float32),
        jnp.zeros(weight_down.shape, jnp.float32),
    )
    qv_total = jnp.zeros((2, local_cols), jnp.float32)
    up_total = jnp.zeros((hidden_cols,), jnp.float32)
    vector_totals = tuple((jnp.zeros((model_width,), jnp.float32) for index_vec in range(6)))
    grad_store = jnp.zeros((slot_count, half_rows, model_width), jnp.bfloat16)
    incoming = jnp.zeros((half_rows, model_width), jnp.bfloat16)
    for step_num in range(micro_count + 1):
        index_mb = step_num - 1 + section_num
        valid_mask = jnp.logical_and(index_mb >= 0, index_mb < micro_count).astype(jnp.float32)
        slot_num = (index_mb + slot_count) % slot_count
        take_num = jnp.clip(index_mb, 0, micro_count - 1)
        given = get_slot(cotangent, take_num)
        grad_out = jnp.where(section_num == 1, given, incoming).astype(jnp.float32)
        batch_ids = get_slot(image_ids, take_num)
        query_ids = lax.dynamic_slice_in_dim(batch_ids, block_num * tok_rows, tok_rows)
        same_image = query_ids[:, None] == batch_ids[None, :]
        rows_now = get_slot(keep_input, slot_num)
        middle = get_slot(keep_middle, slot_num)
        normed = get_slot(keep_normed, slot_num)
        query_low = get_slot(keep_query, slot_num)
        log_total = get_slot(keep_lse, slot_num)
        context = get_slot(keep_context, slot_num)
        feed_input = get_slot(keep_feed, slot_num)
        hidden_state = get_slot(keep_hidden, slot_num)
        keys_all = get_slot(keep_keys, slot_num)
        values_all = get_slot(keep_values, slot_num)
        down_grad = grad_gather(grad_out.astype(jnp.bfloat16))
        active_section = gelu_tanh(hidden_state).astype(jnp.bfloat16)
        grad_down_w = jnp.einsum(
            "rd,rf->df", down_grad, active_section, preferred_element_type=jnp.float32
        )
        active_grad = jnp.dot(down_grad, weight_down, preferred_element_type=jnp.float32)
        gelu_value, gelu_back = jax.vjp(gelu_tanh, hidden_state)
        hidden_grad = gelu_back(active_grad)[0].astype(jnp.bfloat16)
        grad_up_w = jnp.einsum(
            "rd,rf->df", feed_input, hidden_grad, preferred_element_type=jnp.float32
        )
        feed_grad = grad_reduce(contract_last(hidden_grad, weight_up))
        feed_value, feed_back = jax.vjp(normalize, middle, feed_gain, feed_shift)
        middle_part, feed_gain_grad, feed_shift_grad = feed_back(feed_grad)
        middle_grad = grad_out + middle_part
        attn_grad = grad_gather(middle_grad.astype(jnp.bfloat16))
        grad_out_w = jnp.einsum("rd,rj->dj", attn_grad, context, preferred_element_type=jnp.float32)
        context_grad = jnp.dot(attn_grad, weight_out, preferred_element_type=jnp.float32).astype(
            jnp.bfloat16
        )
        scores = head_scores(query_low, keys_all, same_image, heads_local)
        soft_probs = jnp.exp(scores - log_total[:, :, None])
        context_h = context_grad.reshape(tok_rows, heads_local, HD)
        values_h = values_all.reshape(all_rows, heads_local, HD)
        keys_h = keys_all.reshape(all_rows, heads_local, HD)
        query_h = query_low.reshape(tok_rows, heads_local, HD)
        prob_grad = jnp.einsum(
            "qhe,khe->hqk", context_h, values_h, preferred_element_type=jnp.float32
        )
        inner = jnp.sum(soft_probs * prob_grad, axis=-1, keepdims=True)
        score_grad = (soft_probs * (prob_grad - inner)).astype(jnp.bfloat16)
        query_grad = (
            jnp.einsum("hqk,khe->qhe", score_grad, keys_h, preferred_element_type=jnp.float32)
            * score_scale
        )
        query_grad = query_grad.reshape(tok_rows, local_cols).astype(jnp.bfloat16)
        key_part = (
            jnp.einsum("hqk,qhe->khe", score_grad, query_h, preferred_element_type=jnp.float32)
            * score_scale
        ).reshape(all_rows, local_cols)
        value_part = jnp.einsum(
            "hqk,qhe->khe",
            soft_probs.astype(jnp.bfloat16),
            context_h,
            preferred_element_type=jnp.float32,
        ).reshape(all_rows, local_cols)
        key_sum, value_sum = (
            lax.psum_scatter(key_part, "fsdp", scatter_dimension=0, tiled=True),
            lax.psum_scatter(value_part, "fsdp", scatter_dimension=0, tiled=True),
        )
        key_grad = key_sum.astype(jnp.bfloat16)
        value_grad = value_sum.astype(jnp.bfloat16)
        joined = jnp.stack((query_grad, key_grad, value_grad), axis=1)
        grad_in_w = jnp.einsum("rd,rce->dce", normed, joined, preferred_element_type=jnp.float32)
        normed_grad = grad_reduce(
            jnp.einsum("rce,dce->rd", joined, weight_in, preferred_element_type=jnp.float32)
        )
        attn_value, attn_back = jax.vjp(normalize, rows_now, attn_gain, attn_shift)
        rows_part, attn_gain_grad, attn_shift_grad = attn_back(normed_grad)
        input_grad = (middle_grad + rows_part).astype(jnp.bfloat16)
        grad_store = put_slot(grad_store, input_grad, slot_num)
        qv_step = jnp.stack(
            (
                jnp.sum(query_grad.astype(jnp.float32), axis=0),
                jnp.sum(value_grad.astype(jnp.float32), axis=0),
            )
        )
        qv_total = qv_total + valid_mask * qv_step
        up_total = up_total + valid_mask * jnp.sum(hidden_grad.astype(jnp.float32), axis=0)
        vector_steps = (
            jnp.sum(middle_grad, axis=0),
            attn_gain_grad,
            attn_shift_grad,
            jnp.sum(grad_out, axis=0),
            feed_gain_grad,
            feed_shift_grad,
        )
        vector_totals = tuple(
            (
                old_vec + valid_mask * new_vec
                for old_vec, new_vec in zip(vector_totals, vector_steps)
            )
        )
        step_in = valid_mask * grad_in_w
        step_out = valid_mask * grad_out_w
        step_up = valid_mask * grad_up_w
        step_down = valid_mask * grad_down_w
        totals = (
            totals[0] + step_in,
            totals[1] + step_out,
            totals[2] + step_up,
            totals[3] + step_down,
        )
        if step_num < micro_count:
            incoming = from_behind(input_grad, "pipe", -1)
    totals = (
        lax.psum_scatter(totals[0], "fsdp", scatter_dimension=0, tiled=True),
        lax.psum_scatter(totals[1], "fsdp", scatter_dimension=0, tiled=True),
        lax.psum_scatter(totals[2], "fsdp", scatter_dimension=0, tiled=True),
        lax.psum_scatter(totals[3], "fsdp", scatter_dimension=0, tiled=True),
    )
    qv_sum, up_sum = lax.psum((qv_total, up_total), "fsdp")
    vector_sums = lax.psum(
        (
            vector_totals[0],
            vector_totals[1],
            vector_totals[2],
            vector_totals[3],
            vector_totals[4],
            vector_totals[5],
        ),
        ("fsdp", "tp"),
    )
    return (
        act_store[:micro_count][None],
        grad_store[:micro_count][None],
        totals[0][None],
        qv_sum[None],
        totals[1][None],
        vector_sums[0][None],
        vector_sums[1][None],
        vector_sums[2][None],
        totals[2][None],
        up_sum[None],
        totals[3][None],
        vector_sums[3][None],
        vector_sums[4][None],
        vector_sums[5][None],
    )


LANES = 128


def swap_pairs(count, step):
    return [(at, at ^ step) for at in range(count)]


def pick(take_first, first, second):
    return jnp.where(take_first, first, second)


class Plane:
    def __init__(self, planes):
        self.groups = lax.axis_size("fsdp")
        self.planes = planes
        self.across = lax.axis_index("pipe")
        place = lax.axis_index("fsdp")
        self.near = self.groups // planes
        self.plane = place // self.near
        self.side = place % self.near
        self.core = lax.axis_index("tp")
        self.place = jnp.stack((self.plane, self.across, self.side)).astype(jnp.int32)

    def pipe(self, value):
        return lax.ppermute(value, "pipe", [(0, 1), (1, 0)])

    def beside(self, value):
        return lax.ppermute(value, "fsdp", swap_pairs(self.groups, 1))

    def corner(self, value):
        pairs = [
            (one * self.groups + at, (1 - one) * self.groups + (at ^ 1))
            for one in range(2)
            for at in range(self.groups)
        ]
        return lax.ppermute(value, ("pipe", "fsdp"), pairs)

    def core_swap(self, value):
        return lax.ppermute(value, "tp", [(0, 1), (1, 0)])

    def plane_shift(self, value, steps):
        pairs = [(at, (at + steps * self.near) % self.groups) for at in range(self.groups)]
        return lax.ppermute(value, "fsdp", pairs)

    def plane_lists(self):
        return [
            [plane * self.near + side for plane in range(self.planes)] for side in range(self.near)
        ]

    def gather_rows(self, own):
        mine = jnp.concatenate((own, self.pipe(own), self.beside(own), self.corner(own)), axis=0)
        return mine, self.core_swap(mine)

    def reduce_rows(self, kept, sent, beside=()):
        quarter = kept.shape[0] // 4
        low = jnp.bfloat16
        chip = kept + self.core_swap(sent).astype(jnp.float32)
        low_chip = chip.astype(low)
        came = (
            self.pipe(low_chip[quarter : 2 * quarter]),
            self.beside(low_chip[2 * quarter : 3 * quarter]),
            self.corner(low_chip[3 * quarter :]),
        )
        came, beside = lax.optimization_barrier((came, beside))
        total = chip[:quarter]
        for part in came:
            total = total + part.astype(jnp.float32)
        return total, beside

    def absolute(self, parts):
        one, pipe, beside, corner = parts
        first = self.side == 0
        self_0, self_1 = pick(first, one, beside), pick(first, beside, one)
        other_0, other_1 = pick(first, pipe, corner), pick(first, corner, pipe)
        up = self.across == 0
        return (
            pick(up, self_0, other_0),
            pick(up, self_1, other_1),
            pick(up, other_0, self_0),
            pick(up, other_1, self_1),
        )

    def spread_weight(self, parts):
        one, pipe, beside, corner = parts
        pipe, beside, corner = self.pipe(pipe), self.beside(beside), self.corner(corner)
        first = self.side == 0
        same = jnp.concatenate((pick(first, one, beside), pick(first, beside, one)), axis=0)
        other = jnp.concatenate((pick(first, pipe, corner), pick(first, corner, pipe)), axis=0)
        up = self.across == 0
        return pick(up, same, other), pick(up, other, same)

    def gather_planes(self, value):
        return lax.all_gather(
            value, "fsdp", axis=0, tiled=True, axis_index_groups=self.plane_lists()
        )

    def reduce_planes(self, value):
        return lax.psum_scatter(
            value, "fsdp", scatter_dimension=0, tiled=True, axis_index_groups=self.plane_lists()
        )

    def collect_weight(self, first_section, second_section):
        rows = first_section.shape[0] // 2
        up = self.across == 0
        same, other = pick(up, first_section, second_section), pick(up, second_section, first_section)
        first = self.side == 0
        parts = (
            pick(first, same[:rows], same[rows:]),
            self.pipe(pick(first, other[:rows], other[rows:])),
            self.beside(pick(first, same[rows:], same[:rows])),
            self.corner(pick(first, other[rows:], other[:rows])),
        )
        return parts

    def rows_in(self, value):
        got = [lax.dynamic_index_in_dim(value, self.plane, 0, keepdims=False)]
        for steps in range(1, self.planes):
            target = (self.plane + steps) % self.planes
            sent = lax.dynamic_index_in_dim(value, target, 0, keepdims=False)
            got.append(self.plane_shift(sent, steps))
        return self.turned(got)

    def turned(self, got):
        stacked = jnp.stack(got)
        order = [(self.plane + self.planes - at) % self.planes for at in range(self.planes)]
        return jnp.stack(
            [lax.dynamic_index_in_dim(stacked, at, 0, keepdims=False) for at in order]
        )

    def halves(self, value):
        half = self.planes // 2
        flat = value.reshape(2, half * value.shape[1], value.shape[2])
        up = self.across == 0
        return pick(up, flat[0], flat[1]), pick(up, flat[1], flat[0])

    def rows_out(self, first_section, second_section):
        up = self.across == 0
        kept = pick(up, first_section, second_section)
        came = self.pipe(pick(up, second_section, first_section))
        both = jnp.concatenate((pick(up, kept, came), pick(up, came, kept)), axis=0)
        blocks = both.reshape(self.planes, both.shape[0] // self.planes, both.shape[1])
        return self.rows_in(blocks)


def norm_parts(values):
    row_mean = jnp.mean(values, axis=-1, keepdims=True)
    center = values - row_mean
    spread = jnp.mean(center * center, axis=-1, keepdims=True)
    scale = lax.rsqrt(spread + EPSILON)
    return center * scale, scale


def norm_forward(values, gain_vec, shift_vec):
    return norm_parts(values)[0] * gain_vec + shift_vec


def norm_backward(values, gain_vec, grad):
    shape, scale = norm_parts(values)
    inner = grad * gain_vec
    mean_one = jnp.mean(inner, axis=-1, keepdims=True)
    mean_two = jnp.mean(inner * shape, axis=-1, keepdims=True)
    back = (inner - mean_one - shape * mean_two) * scale
    return back, jnp.sum(grad * shape, axis=0), jnp.sum(grad, axis=0)


def gelu_both(values):
    root = (2.0 / jnp.pi) ** 0.5
    square = values * values
    inside = jnp.tanh(root * values * (1.0 + 0.044715 * square))
    value = 0.5 * values * (1.0 + inside)
    slope = 0.5 * (1.0 + inside) + 0.5 * values * (1.0 - inside * inside) * root * (
        1.0 + 3.0 * 0.044715 * square
    )
    return value, slope


VMEM_LIMIT = 60 * 1024 * 1024
NT = (((1,), (1,)), ((), ()))
TN = (((0,), (0,)), ((), ()))


def dot_of(left, right, dims):
    return lax.dot_general(left, right, dims, preferred_element_type=jnp.float32)


def kernel_call(body_of, name, outs, flops, moved, *args, scratch=(), scalars=None):
    specs = [pl.BlockSpec(memory_space=pltpu.VMEM)] * len(args)
    if scalars is not None:
        specs, args = [pl.BlockSpec(memory_space=pltpu.SMEM)] + specs, (scalars,) + args
    return pl.pallas_call(
        body_of,
        name=name,
        out_shape=[jax.ShapeDtypeStruct(shape, kind) for shape, kind in outs],
        in_specs=specs,
        out_specs=[pl.BlockSpec(memory_space=pltpu.VMEM)] * len(outs),
        scratch_shapes=list(scratch),
        compiler_params=pltpu.CompilerParams(vmem_limit_bytes=VMEM_LIMIT),
        cost_estimate=pl.CostEstimate(flops=flops, bytes_accessed=moved, transcendentals=0),
    )(*args)


def chosen(index, values):
    found = values[-1]
    for at in range(len(values) - 2, -1, -1):
        found = jnp.where(index == at, values[at], found)
    return found


def share_of(place, relative):
    across = place[1] if relative % 2 == 0 else 1 - place[1]
    side = place[2] if relative < 2 else 1 - place[2]
    return across * 2 + side


def relative_of(place, share):
    across, side = share // 2, share % 2
    pipe_step = jnp.where(place[1] == across, 0, 1)
    side_step = jnp.where(place[2] == side, 0, 1)
    return side_step * 2 + pipe_step


def pack_attn_kernel(place, proj_in, proj_out, *outs):
    own = outs[0].shape[1] // 4
    parts = [proj_in[0], proj_in[1], proj_in[2], proj_out[...]]
    shares = [
        jnp.concatenate([part[:, at * own : (at + 1) * own] for part in parts], axis=1) for at in range(len(outs))
    ]
    for relative, out in enumerate(outs):
        out[...] = chosen(share_of(place, relative), shares)


def pack_feed_kernel(place, up, down, *outs):
    own = outs[0].shape[1] // 2
    shares = [
        jnp.concatenate([part[:, at * own : (at + 1) * own] for part in (up, down)], axis=1)
        for at in range(len(outs))
    ]
    for relative, out in enumerate(outs):
        out[...] = chosen(share_of(place, relative), shares)


def unpack_attn_kernel(place, *refs):
    parts, (grad_in, grad_out) = refs[:-2], refs[-2:]
    own = parts[0].shape[1] // 4
    values = [part[...].astype(jnp.float32) for part in parts]
    ordered = [chosen(relative_of(place, share), values) for share in range(len(parts))]
    for at in range(4):
        joined = jnp.concatenate([one[:, at * own : (at + 1) * own] for one in ordered], axis=1)
        if at < 3:
            grad_in[at] = joined
        else:
            grad_out[...] = joined


def unpack_feed_kernel(place, *refs):
    parts, outs = refs[:-2], refs[-2:]
    own = parts[0].shape[1] // 2
    values = [part[...].astype(jnp.float32) for part in parts]
    ordered = [chosen(relative_of(place, share), values) for share in range(len(parts))]
    for at, out in enumerate(outs):
        out[...] = jnp.concatenate([one[:, at * own : (at + 1) * own] for one in ordered], axis=1)


def wide_head(value, at):
    part = value[:, at * HD : (at + 1) * HD]
    return jnp.concatenate((part, jnp.zeros((part.shape[0], LANES - HD), part.dtype)), axis=1)


def head_probs(query, keys, rows_ids, all_ids):
    scores = dot_of(query, keys, NT) * HD ** (-0.5)
    scores = jnp.where(rows_ids == all_ids, scores, MASKED)
    exp_scores = jnp.exp(scores - jnp.max(scores, axis=-1, keepdims=True))
    return exp_scores / jnp.sum(exp_scores, axis=-1, keepdims=True)


def lane(at):
    return slice(at * LANES, (at + 1) * LANES)


def attn_kernel(heads, mine, other, weight, bias, ids_col, ids_row, wide, context, kept, sent):
    low = jnp.bfloat16
    half = mine.shape[0]
    cols = 3 * heads * HD
    into = weight[:, :cols]
    for part, rows in enumerate((mine, other)):
        projected = dot_of(rows[...], into, (((1,), (0,)), ((), ()))) + bias[...]
        for at in range(3 * heads):
            wide[part * half : (part + 1) * half, lane(at)] = wide_head(projected, at).astype(low)
    out = weight[:, cols:]
    for part in range(2):
        span = slice(part * half, (part + 1) * half)
        found = []
        for at in range(heads):
            probs = head_probs(wide[span, lane(at)], wide[:, lane(heads + at)], ids_col[span], ids_row[...])
            one = dot_of(probs.astype(low), wide[:, lane(2 * heads + at)], (((1,), (0,)), ((), ())))
            found.append(one[:, :HD])
        joined = jnp.concatenate(found, axis=1).astype(low)
        context[span] = joined
        result = dot_of(joined, out, NT)
        if part == 0:
            kept[...] = result
        else:
            sent[...] = result.astype(low)


def attn_back_kernel(heads, mine, other, weight, wide, ids_col, ids_row, joined, kept, sent, sums, wide_grad, key_sum, value_sum):
    low = jnp.bfloat16
    half = mine.shape[0]
    cols = 3 * heads * HD
    out = weight[:, cols:]
    scale = HD ** (-0.5)
    for part, rows in enumerate((mine, other)):
        grad = dot_of(rows[...], out, (((1,), (0,)), ((), ())))
        for at in range(heads):
            wide_grad[part * half : (part + 1) * half, lane(at)] = wide_head(grad, at).astype(low)
    for part in range(2):
        span = slice(part * half, (part + 1) * half)
        for at in range(heads):
            query, keys, values = wide[span, lane(at)], wide[:, lane(heads + at)], wide[:, lane(2 * heads + at)]
            probs = head_probs(query, keys, ids_col[span], ids_row[...])
            context_grad = wide_grad[span, lane(at)]
            prob_grad = dot_of(context_grad, values, NT)
            inner = jnp.sum(probs * prob_grad, axis=-1, keepdims=True)
            score_grad = (probs * (prob_grad - inner)).astype(low)
            query_grad = dot_of(score_grad, keys, (((1,), (0,)), ((), ()))) * scale
            joined[span, at * HD : (at + 1) * HD] = query_grad[:, :HD].astype(low)
            key_part = dot_of(score_grad, query, TN)
            value_part = dot_of(probs.astype(low), context_grad, TN)
            if part == 0:
                key_sum[:, lane(at)] = key_part
                value_sum[:, lane(at)] = value_part
            else:
                key_part = (key_sum[:, lane(at)] + key_part) * scale
                value_part = value_sum[:, lane(at)] + value_part
                joined[:, (heads + at) * HD : (heads + at + 1) * HD] = key_part[:, :HD].astype(low)
                joined[:, (2 * heads + at) * HD : (2 * heads + at + 1) * HD] = value_part[:, :HD].astype(low)
    into = weight[:, :cols]
    total = jnp.zeros((1, cols), jnp.float32)
    for part in range(2):
        rows = joined[part * half : (part + 1) * half]
        total = total + jnp.sum(rows.astype(jnp.float32), axis=0, keepdims=True)
        result = dot_of(rows, into, NT)
        if part == 0:
            kept[...] = result
        else:
            sent[...] = result.astype(low)
    sums[...] = total


def feed_kernel(mine, other, weight, bias, hidden, kept, sent):
    low = jnp.bfloat16
    half = mine.shape[0]
    hidden_cols = weight.shape[1] // 2
    up, down = weight[:, :hidden_cols], weight[:, hidden_cols:]
    for part, rows in enumerate((mine, other)):
        value = dot_of(rows[...], up, (((1,), (0,)), ((), ()))) + bias[...]
        hidden[part * half : (part + 1) * half] = value
        result = dot_of(gelu_both(value)[0].astype(low), down, NT)
        if part == 0:
            kept[...] = result
        else:
            sent[...] = result.astype(low)


def feed_back_kernel(mine, other, weight, hidden, hidden_grad, active, kept, sent, sums):
    low = jnp.bfloat16
    half = mine.shape[0]
    hidden_cols = weight.shape[1] // 2
    up, down = weight[:, :hidden_cols], weight[:, hidden_cols:]
    total = jnp.zeros(sums.shape, jnp.float32)
    for part, rows in enumerate((mine, other)):
        span = slice(part * half, (part + 1) * half)
        value, slope = gelu_both(hidden[span])
        active[span] = value.astype(low)
        grad = (dot_of(rows[...], down, (((1,), (0,)), ((), ()))) * slope).astype(low)
        hidden_grad[span] = grad
        total = total + jnp.sum(grad.astype(jnp.float32), axis=0, keepdims=True)
        result = dot_of(grad, up, NT)
        if part == 0:
            kept[...] = result
        else:
            sent[...] = result.astype(low)
    sums[...] = total


def feed_weight_kernel(feed_mine, feed_other, given_mine, given_other, hidden_grad, active, out):
    half = feed_mine.shape[0]
    for tile in range(feed_mine.shape[1] // LANES):
        one = dot_of(feed_mine[:, lane(tile)], hidden_grad[:half], TN)
        one = one + dot_of(feed_other[:, lane(tile)], hidden_grad[half:], TN)
        two = dot_of(given_mine[:, lane(tile)], active[:half], TN)
        two = two + dot_of(given_other[:, lane(tile)], active[half:], TN)
        out[lane(tile)] = jnp.concatenate((one, two), axis=1).astype(jnp.bfloat16)


def attn_weight_kernel(normed_mine, normed_other, grad_mine, grad_other, joined, context, out):
    half = normed_mine.shape[0]
    for tile in range(normed_mine.shape[1] // LANES):
        one = dot_of(normed_mine[:, lane(tile)], joined[:half], TN)
        one = one + dot_of(normed_other[:, lane(tile)], joined[half:], TN)
        two = dot_of(grad_mine[:, lane(tile)], context[:half], TN)
        two = two + dot_of(grad_other[:, lane(tile)], context[half:], TN)
        out[lane(tile)] = jnp.concatenate((one, two), axis=1).astype(jnp.bfloat16)


class Section:
    def __init__(self, plane, heads, weights, vectors, ids_col, ids_row):
        self.plane = plane
        self.heads = heads
        self.attn, self.feed_weight = weights
        self.ids_col, self.ids_row = ids_col, ids_row
        (
            self.attn_bias,
            self.up_bias,
            self.out_bias,
            self.gain_attn,
            self.shift_attn,
            self.down_bias,
            self.gain_feed,
            self.shift_feed,
        ) = vectors

    def norm_attn(self, rows):
        return norm_forward(rows, self.gain_attn, self.shift_attn).astype(jnp.bfloat16)

    def sizes(self, normed):
        count, width = 2 * normed[0].shape[0], normed[0].shape[1]
        return count, width, self.heads * HD, self.feed_weight.shape[1] // 2

    def halves(self, width, count):
        return [((count // 2, width), jnp.float32), ((count // 2, width), jnp.bfloat16)]

    def forward(self, rows, normed):
        plane, heads = self.plane, self.heads
        low = jnp.bfloat16
        count, width, own, hidden = self.sizes(normed)
        self.rows, self.normed = rows, normed
        self.wide, self.context, kept, sent = kernel_call(
            functools.partial(attn_kernel, heads),
            "attn_forward",
            [((count, 3 * heads * LANES), low), ((count, own), low)] + self.halves(width, count),
            2 * count * own * (4 * width + 2 * count),
            2 * (count + 4 * own) * width + 6 * count * width,
            *normed,
            self.attn,
            self.attn_bias,
            self.ids_col,
            self.ids_row,
        )
        attended, _ = plane.reduce_rows(kept, sent)
        self.middle = rows + attended + self.out_bias
        feed = norm_forward(self.middle, self.gain_feed, self.shift_feed).astype(low)
        self.feed = plane.gather_rows(feed)
        self.hidden, kept, sent = kernel_call(
            feed_kernel,
            "feed_forward",
            [((count, hidden), jnp.float32)] + self.halves(width, count),
            4 * count * width * hidden,
            2 * (count + 2 * hidden) * width + 6 * count * width,
            *self.feed,
            self.feed_weight,
            self.up_bias,
        )
        fed, _ = plane.reduce_rows(kept, sent)
        return (self.middle + fed + self.down_bias).astype(low)

    def backward(self, grad, gathered, before=((), ())):
        plane, heads = self.plane, self.heads
        low = jnp.bfloat16
        count, width, own, hidden = self.sizes(self.normed)
        hidden_grad, active, kept, sent, grad_up_bias = kernel_call(
            feed_back_kernel,
            "feed_backward",
            [((count, hidden), low)] * 2 + self.halves(width, count) + [((1, hidden), jnp.float32)],
            4 * count * width * hidden,
            2 * (count + 2 * hidden) * width + 6 * count * width,
            *gathered,
            self.feed_weight,
            self.hidden,
        )
        (grad_feed,) = kernel_call(
            feed_weight_kernel,
            "feed_weights",
            [(self.feed_weight.shape, low)],
            4 * count * width * hidden,
            4 * (count + hidden) * width,
            *self.feed,
            *gathered,
            hidden_grad,
            active,
        )
        feed_grad, (grad_feed,) = plane.reduce_rows(kept, sent, (grad_feed,))
        feed_shard = plane.reduce_planes(grad_feed)
        back, grad_gain_feed, grad_shift_feed = norm_backward(self.middle, self.gain_feed, feed_grad)
        middle_grad = grad + back
        low_middle, early = lax.optimization_barrier((middle_grad.astype(low), before[0]))
        attn_grad = plane.gather_rows(low_middle)
        joined, kept, sent, bias_sums = kernel_call(
            functools.partial(attn_back_kernel, heads),
            "attn_backward",
            [((count, 3 * own), low)] + self.halves(width, count) + [((1, 3 * own), jnp.float32)],
            2 * count * own * (4 * width + 5 * count),
            2 * (count + 4 * own) * width + 6 * count * width,
            *attn_grad,
            self.attn,
            self.wide,
            self.ids_col,
            self.ids_row,
            scratch=[
                pltpu.VMEM((count, heads * LANES), low),
                pltpu.VMEM((count, heads * LANES), jnp.float32),
                pltpu.VMEM((count, heads * LANES), jnp.float32),
            ],
        )
        (grad_attn,) = kernel_call(
            attn_weight_kernel,
            "attn_weights",
            [(self.attn.shape, low)],
            2 * count * width * 4 * own,
            4 * (count + 2 * own) * width,
            *self.normed,
            *attn_grad,
            joined,
            self.context,
        )
        normed_grad, (grad_attn,) = plane.reduce_rows(kept, sent, (grad_attn,))
        attn_shard = plane.reduce_planes(grad_attn)
        normed_grad, late = lax.optimization_barrier((normed_grad, before[1]))
        rows_back, grad_gain_attn, grad_shift_attn = norm_backward(self.rows, self.gain_attn, normed_grad)
        result = (middle_grad + rows_back).astype(low)
        sums = (
            jnp.sum(middle_grad, axis=0),
            grad_gain_attn,
            grad_shift_attn,
            jnp.sum(grad, axis=0),
            grad_gain_feed,
            grad_shift_feed,
        )
        columns = jnp.concatenate((bias_sums[0, :own], bias_sums[0, 2 * own :], grad_up_bias[0]))
        return result, (attn_shard, feed_shard), sums, columns, (early, late)


def plane_body(
    inputs,
    cotangent,
    image_ids,
    proj_in,
    bias_in,
    proj_out,
    bias_out,
    gain_attn,
    shift_attn,
    up_projection,
    up_bias_vector,
    down_projection,
    bias_down,
    gain_feed,
    shift_feed,
):
    micro_count, part_rows, model_width = inputs.shape
    local_cols = proj_in.shape[3]
    hidden_cols = up_projection.shape[2]
    shard_rows = proj_in.shape[1]
    plane = Plane(micro_count)
    shares = 4
    own_cols = local_cols // shares
    own_hidden = hidden_cols // shares
    heads = own_cols // HD
    up = plane.across == 0
    share_num = plane.across * 2 + plane.side

    low = jnp.bfloat16
    attn_parts = kernel_call(
        pack_attn_kernel,
        "pack_attn",
        [((shard_rows, 4 * own_cols), low)] * shares,
        0,
        32 * shard_rows * own_cols,
        proj_in[0].transpose(1, 0, 2),
        proj_out[0],
        scalars=plane.place,
    )

    tail = -hidden_cols % model_width
    bias_row = jnp.concatenate((bias_in[0, :1], bias_in[0, 1:]), axis=1)
    hidden_rows = jnp.pad(up_bias_vector, ((0, 0), (0, tail))).reshape(-1, model_width)
    vec = jnp.concatenate(
        (bias_row, bias_out, gain_attn, shift_attn, bias_down, gain_feed, shift_feed, hidden_rows), axis=0
    )
    attn_parts, vec, inputs = lax.optimization_barrier((attn_parts, vec, inputs))
    attn_pair = plane.spread_weight(attn_parts)
    vec_other = plane.pipe(vec)
    rows_all = plane.rows_in(inputs)

    rows_all, attn_pair, up_projection, down_projection = lax.optimization_barrier(
        (rows_all, attn_pair, up_projection, down_projection)
    )
    feed_parts = kernel_call(
        pack_feed_kernel,
        "pack_feed",
        [((shard_rows, 2 * own_hidden), low)] * shares,
        0,
        16 * shard_rows * own_hidden,
        up_projection[0],
        down_projection[0],
        scalars=plane.place,
    )
    feed_pair = plane.spread_weight(feed_parts)

    vec_both = pick(up, jnp.stack((vec, vec_other)), jnp.stack((vec_other, vec))).astype(jnp.float32)
    zero = jnp.zeros((2, own_cols), jnp.float32)
    query_both = lax.dynamic_slice(vec_both, (0, 0, share_num * own_cols), (2, 1, own_cols))[:, 0]
    value_both = lax.dynamic_slice(vec_both, (0, 0, local_cols + share_num * own_cols), (2, 1, own_cols))[:, 0]
    bias_both = jnp.concatenate((query_both, zero, value_both), axis=1)
    hidden_both = lax.dynamic_slice(vec_both[:, 7:].reshape(2, -1), (0, share_num * own_hidden), (2, own_hidden))

    def vectors(section):
        wide = vec_both[section, 1:7]
        return (bias_both[section : section + 1], hidden_both[section : section + 1]) + tuple(
            wide[at : at + 1] for at in range(6)
        )

    ids = lax.dynamic_index_in_dim(image_ids, plane.plane, 0, keepdims=False)
    ids = ids.reshape(2, micro_count // 2, 2, 2, part_rows)
    ids = pick(up, ids, jnp.flip(ids, 0))
    ids = pick(plane.side == 0, ids, jnp.flip(ids, 2))
    ids = pick(plane.core == 0, ids, jnp.flip(ids, 3))
    ids = ids.transpose(3, 2, 0, 1, 4).reshape(-1)
    ids_col, ids_row = ids[:, None], ids[None, :]

    own_rows, pair_rows = plane.halves(rows_all)
    pair_float = jnp.concatenate((own_rows, pair_rows), axis=0).astype(jnp.float32)
    vector_sets = [vectors(section) for section in range(2)]
    pair_normed = norm_forward(pair_float, vector_sets[0][3], vector_sets[0][4]).astype(jnp.bfloat16)
    mine = jnp.concatenate((pair_normed, plane.beside(pair_normed)), axis=0)
    normed = (mine, plane.core_swap(mine))
    first_attn = plane.gather_planes(attn_pair[0])
    first_feed = plane.gather_planes(feed_pair[0])
    normed, attn_second, feed_second = lax.optimization_barrier((normed, attn_pair[1], feed_pair[1]))
    second_attn, second_feed = plane.gather_planes(attn_second), plane.gather_planes(feed_second)
    sections = [
        Section(plane, heads, weights, vector_sets[at], ids_col, ids_row)
        for at, weights in enumerate(((first_attn, first_feed), (second_attn, second_feed)))
    ]
    result = []
    rows = own_rows
    for section in range(2):
        one = sections[section]
        rows = rows.astype(jnp.float32)
        if section > 0:
            normed = plane.gather_rows(one.norm_attn(rows))
        rows = one.forward(rows, normed)
        result.append(rows)

    given = plane.rows_in(cotangent)
    own_given, pair_given = plane.halves(given)
    pair = jnp.concatenate((own_given, pair_given), axis=0)
    mine = jnp.concatenate((pair, plane.beside(pair)), axis=0)
    gathered = (mine, plane.core_swap(mine))
    grad = own_given
    back = [None, None]
    weight_grads, sums, columns = [None, None], [None, None], [None, None]
    for section in (1, 0):
        if section == 0:
            gathered = plane.gather_rows(grad)
        before = ((weight_grads[1][1],), (weight_grads[1][0],)) if section == 0 else ((), ())
        grad, weight_grads[section], sums[section], columns[section], held = sections[section].backward(
            grad.astype(jnp.float32), gathered, before
        )
        if section == 0:
            weight_grads[1] = (held[1][0], held[0][0])
        back[section] = grad

    activations = plane.rows_out(result[0], result[1])
    grad_inputs = plane.rows_out(back[0], back[1])
    blocks = [
        plane.collect_weight(one, two) for one, two in zip(weight_grads[0], weight_grads[1])
    ]
    grad_in, grad_out = kernel_call(
        unpack_attn_kernel,
        "unpack_attn",
        [((3, shard_rows, local_cols), jnp.float32), ((shard_rows, local_cols), jnp.float32)],
        0,
        24 * shard_rows * local_cols,
        *blocks[0],
        scalars=plane.place,
    )
    grad_in = grad_in.transpose(1, 0, 2)
    grad_up, grad_down = kernel_call(
        unpack_feed_kernel,
        "unpack_feed",
        [((shard_rows, hidden_cols), jnp.float32)] * 2,
        0,
        12 * shard_rows * hidden_cols,
        *blocks[1],
        scalars=plane.place,
    )

    column_count = columns[0].shape[0]
    pad = -column_count % model_width
    packs = [
        jnp.concatenate(sums[section] + (columns[section], jnp.zeros((pad,), jnp.float32))).reshape(-1, model_width)
        for section in range(2)
    ]
    pack = jnp.concatenate(packs, axis=0)
    both = pack + plane.core_swap(pack)
    per = packs[0].shape[0]
    rolled = jnp.stack([both[:6], both[per : per + 6]])
    held = jnp.stack([pack[6:per], pack[per + 6 :]])
    message = jnp.concatenate((rolled, held), axis=1)
    send_same = pick(up, message[0], message[1])
    send_other = pick(up, message[1], message[0])
    parts = (send_same, plane.pipe(send_other), plane.beside(send_same), plane.corner(send_other))
    ordered = plane.absolute(parts)
    total = parts[0][:6] + parts[1][:6] + parts[2][:6] + parts[3][:6]
    kept = jnp.concatenate([total] + [part[6:] for part in ordered], axis=0)
    full = kept
    for steps in range(1, plane.planes):
        full = full + plane.plane_shift(kept, steps)
    parts = full[6:].reshape(shares, -1)[:, :column_count]
    grad_bias_in = jnp.stack(
        (parts[:, :own_cols].reshape(-1), parts[:, own_cols : 2 * own_cols].reshape(-1))
    )
    grad_up_bias = parts[:, 2 * own_cols :].reshape(-1)
    return (
        activations[None],
        grad_inputs[None],
        grad_in[None],
        grad_bias_in[None],
        grad_out[None],
        full[0][None],
        full[1][None],
        full[2][None],
        grad_up[None],
        grad_up_bias[None],
        grad_down[None],
        full[3][None],
        full[4][None],
        full[5][None],
    )


def fits_planes(inputs, proj_in, up_projection):
    micro_count = inputs.shape[0]
    return (
        lax.axis_size("pipe") == 2
        and lax.axis_size("tp") == 2
        and micro_count % 2 == 0
        and lax.axis_size("fsdp") == 2 * micro_count
        and proj_in.shape[3] % (4 * HD) == 0
        and up_projection.shape[2] % 4 == 0
    )


def choose(inputs, cotangent, image_ids, proj_in, *rest):
    form = plane_body if fits_planes(inputs, proj_in, rest[5]) else body
    return form(inputs, cotangent, image_ids, proj_in, *rest)


def solution(mesh):
    placed = (
        P(None, ("fsdp", "tp"), None),
        P(None, ("fsdp", "tp"), None),
        P(),
        P("pipe", "fsdp", None, "tp"),
        P("pipe", None, "tp"),
        P("pipe", "fsdp", "tp"),
        P("pipe", None),
        P("pipe", None),
        P("pipe", None),
        P("pipe", "fsdp", "tp"),
        P("pipe", "tp"),
        P("pipe", "fsdp", "tp"),
        P("pipe", None),
        P("pipe", None),
        P("pipe", None),
    )
    return jax.shard_map(
        choose,
        mesh=mesh,
        in_specs=placed,
        out_specs=(
            P("pipe", None, ("fsdp", "tp"), None),
            P("pipe", None, ("fsdp", "tp"), None),
            P("pipe", "fsdp", None, "tp"),
            P("pipe", None, "tp"),
            P("pipe", "fsdp", "tp"),
            P("pipe", None),
            P("pipe", None),
            P("pipe", None),
            P("pipe", "fsdp", "tp"),
            P("pipe", "tp"),
            P("pipe", "fsdp", "tp"),
            P("pipe", None),
            P("pipe", None),
            P("pipe", None),
        ),
        check_vma=False,
    )
```
